32 devices in a mesh: parts: 2 (over y), mp: 4 (over z), shot: 4 (over x, core).
Axes of the slice: x: 2, y: 2, z: 4, core: 2. Of those that a mesh axis runs over, the one named last changes fastest.
Arguments:
- courant: float32 [192, 256, 128], P(('parts', 'mp')), parts along dimension 0, may hold values from 0.04 to 0.2
- forward_old: float32 [8, 96, 256, 128], P(('parts', 'shot'), 'mp'), parts along dimension 0, may hold values from -5 to 5
- forward_now: float32 [8, 96, 256, 128], P(('parts', 'shot'), 'mp'), parts along dimension 0, may hold values from -5 to 5
- adjoint_late: float32 [8, 96, 256, 128], P(('parts', 'shot'), 'mp'), parts along dimension 0, may hold values from -5 to 5
- adjoint_now: float32 [8, 96, 256, 128], P(('parts', 'shot'), 'mp'), parts along dimension 0, may hold values from -5 to 5
- src_cell: int32 [8, 64], P(('parts', 'shot')), parts along dimension 0, may hold values from 0 to 3145727
- src_sign: int32 [8, 64], P(('parts', 'shot')), parts along dimension 0, may hold values from 0 to 1
- wavelet: float32 [8, 2, 64], P(('parts', 'shot')), parts along dimension 0, may hold values from -16 to 16
- rec_cell: int32 [4096], P('parts'), parts along dimension 0, may hold values from 0 to 3145727
- rec_data: float32 [8, 2, 2048], P(('parts', 'shot')), parts along dimension 0, may hold values from -16 to 16
Outputs:
- raw_gradient: float32 [192, 256, 128], P(('parts', 'mp'), 'shot'), parts along dimension 0
- smooth_gradient: float32 [192, 256, 128], P(('parts', 'shot'), None, 'mp'), parts along dimension 0
The draws below stay inside these ranges and needn't reach their ends.
There are 2 independent parts, one for each index of `parts`. The reference program is written for one: setup_inputs(seed, part) draws one part's arguments, and reference() takes and returns one part's arrays. A program takes and returns all parts, laid end to end along the dimension named above; each array names one. Nothing has to cross between parts.
All inputs are finite; a program needn't handle non-finite values.
Results may differ from the reference program's by a relative error of at most 0.00025.
Values sent between devices are 32-bit elements; how exact they have to be, the bound alone decides.
A program may use at most 128 MiB of HBM per device.

```python
import math
import jax
import jax.numpy as jnp
from jax import lax

NY = 256
NZ = 128
NSRC = 64
NREC = 2048
SMOOTH_X = 32
SMOOTH_YZ = 4
NX = 96
SHOTS = 4


def set_ends(array, own_key, low, top_value):
    place = [jax.random.randint(jax.random.fold_in(own_key, axis), (), 0, length) for axis, length in enumerate(array.shape)]
    widest = array.shape.index(max(array.shape))
    next_to = place[:widest] + [(place[widest] + 1) % array.shape[widest]] + place[widest + 1:]
    return array.at[tuple(place)].set(low).at[tuple(next_to)].set(top_value)


def steps_of(rng, shape, split, low, high):
    level, own = 1.0, jax.random.fold_in(rng, 6)
    for dim, blocks in split:
        steps = jnp.exp(jax.random.uniform(jax.random.fold_in(own, dim), (blocks,), jnp.float32, low / len(split), high / len(split)))
        level = level * jnp.repeat(steps, shape[dim] // blocks).reshape([-1 if axis == dim else 1 for axis in range(len(shape))])
    return level


def normal_values(own_key, dims, spread, most, shards=(), held_as=jnp.bfloat16):
    entries = jax.random.normal(own_key, dims, jnp.float32) * spread
    if len(shards) > 0:
        entries = steps_of(own_key, dims, shards, -0.22, 0.18) * entries
    return jnp.clip(entries, min=-most, max=most).astype(held_as)


def setup_inputs(seed: int = 0, part: int = 0) -> dict:
    seeds = jax.random.split(jax.random.key(seed), 11)
    own_keys = jax.random.split(jax.random.fold_in(seeds[10], part), 11)
    return {
        "courant": jnp.clip(jnp.exp(math.log(0.2) - 1.609438 * jax.random.uniform(own_keys[0], (NX, NY, NZ), jnp.float32) ** steps_of(own_keys[0], (NX, NY, NZ), ((0, 4),), -0.2, 0.2)), 0.04, 0.2),
        "forward_old": normal_values(own_keys[1], (SHOTS, NX, NY, NZ), 0.7, 5.0, ((0, 4), (1, 4)), jnp.float32),
        "forward_now": normal_values(own_keys[2], (SHOTS, NX, NY, NZ), 0.7, 5.0, ((0, 4), (1, 4)), jnp.float32),
        "adjoint_late": normal_values(own_keys[3], (SHOTS, NX, NY, NZ), 0.7, 5.0, ((0, 4), (1, 4)), jnp.float32),
        "adjoint_now": normal_values(own_keys[4], (SHOTS, NX, NY, NZ), 0.7, 5.0, ((0, 4), (1, 4)), jnp.float32),
        "src_cell": set_ends(jax.random.randint(own_keys[5], (SHOTS, NSRC), 0, NX * NY * NZ), jax.random.fold_in(own_keys[5], 1), 0, (NX * NY * NZ) - 1).astype(jnp.int32),
        "src_sign": set_ends(jax.random.randint(own_keys[6], (SHOTS, NSRC), 0, 2), jax.random.fold_in(own_keys[6], 1), 0, 1).astype(jnp.int32),
        "wavelet": normal_values(own_keys[7], (SHOTS, 2, NSRC), 4.0, 16.0, ((0, 4),), jnp.float32),
        "rec_cell": set_ends(jax.random.randint(own_keys[8], (NREC,), 0, NX * NY * NZ), jax.random.fold_in(own_keys[8], 1), 0, (NX * NY * NZ) - 1).astype(jnp.int32),
        "rec_data": normal_values(own_keys[9], (SHOTS, 2, NREC), 4.0, 16.0, ((0, 4),), jnp.float32),
    }


COEFS = (8.0 / 5.0, -1.0 / 5.0, 8.0 / 315.0, -1.0 / 560.0)
CENTER = -205.0 / 72.0

def laplace(padded):
    row_count = padded.shape[-3] - 8
    center_rows = padded[..., 4:4 + row_count, :, :]
    leading = ((0, 0),) * (padded.ndim - 3)
    padded_yz = jnp.pad(center_rows, leading + ((0, 0), (4, 4), (4, 4)))
    width_y = center_rows.shape[-2]
    width_z = center_rows.shape[-1]
    accum_sum = 3.0 * CENTER * center_rows
    for offset, weight in enumerate(COEFS):
        reach = offset + 1
        along_x = padded[..., 4 + reach:4 + reach + row_count, :, :] + padded[..., 4 - reach:4 - reach + row_count, :, :]
        along_y = padded_yz[..., :, 4 + reach:4 + reach + width_y, 4:4 + width_z] + padded_yz[..., :, 4 - reach:4 - reach + width_y, 4:4 + width_z]
        along_z = padded_yz[..., :, 4:4 + width_y, 4 + reach:4 + reach + width_z] + padded_yz[..., :, 4:4 + width_y, 4 - reach:4 - reach + width_z]
        accum_sum = accum_sum + weight * (along_x + along_y + along_z)
    return accum_sum

def inject(field, cells, values, first_row):
    plane_size = field.shape[-2] * field.shape[-1]
    local_cell = cells - first_row * plane_size
    valid = (local_cell >= 0) & (local_cell < field.size)
    target = jnp.where(valid, local_cell, field.size)
    return field.reshape(-1).at[target].add(values, mode='drop').reshape(field.shape)

def sine_table(length):
    counter = jnp.arange(length, dtype=jnp.int32) + 1
    product = counter[:, None] * counter[None, :] % (2 * (length + 1))
    return jnp.sin(jnp.pi * product.astype(jnp.float32) / (length + 1))

def response(length, strength):
    counter = jnp.arange(length, dtype=jnp.int32) + 1
    half_sine = jnp.sin(jnp.pi * counter.astype(jnp.float32) / (2 * (length + 1)))
    return 1.0 / (1.0 + strength * 4.0 * half_sine * half_sine)

def spread_scale(fx_resp, fy_resp, fz_resp):
    return 1.0 / jnp.sqrt(jnp.mean(fx_resp * fx_resp)) * (1.0 / jnp.sqrt(jnp.mean(fy_resp * fy_resp))) * (1.0 / jnp.sqrt(jnp.mean(fz_resp * fz_resp)))

def pad_rows(field):
    return jnp.pad(field, ((4, 4), (0, 0), (0, 0)))

def reference(courant, forward_old, forward_now, adjoint_late, adjoint_now, src_cell, src_sign, wavelet, rec_cell, rec_data):
    total_sum = jnp.zeros(courant.shape, jnp.float32)
    for group in range(SHOTS):
        signed = (2 * src_sign[group] - 1).astype(jnp.float32)
        now_fwd = forward_now[group]
        now_adj = adjoint_now[group]
        accel_first = inject(courant * laplace(pad_rows(now_fwd)), src_cell[group], signed * wavelet[group, 0], 0)
        next_fwd = 2.0 * now_fwd - forward_old[group] + accel_first
        accel_second = inject(courant * laplace(pad_rows(next_fwd)), src_cell[group], signed * wavelet[group, 1], 0)
        mid_adj = 2.0 * now_adj - adjoint_late[group] + inject(courant * laplace(pad_rows(now_adj)), rec_cell, rec_data[group, 0], 0)
        first_adj = 2.0 * mid_adj - now_adj + inject(courant * laplace(pad_rows(mid_adj)), rec_cell, rec_data[group, 1], 0)
        total_sum = total_sum + (first_adj * accel_first + mid_adj * accel_second)
    raw_gradient = total_sum / SHOTS
    highest = lax.Precision.HIGHEST
    table_x = sine_table(NX)
    table_y = sine_table(NY)
    table_z = sine_table(NZ)
    fx_resp = response(NX, float(SMOOTH_X * SMOOTH_X))
    fy_resp = response(NY, float(SMOOTH_YZ * SMOOTH_YZ))
    fz_resp = response(NZ, float(SMOOTH_YZ * SMOOTH_YZ))
    spectrum = jnp.einsum('ia,abc->ibc', table_x, raw_gradient, precision=highest)
    spectrum = jnp.einsum('jb,ibc->ijc', table_y, spectrum, precision=highest)
    spectrum = jnp.einsum('kc,ijc->ijk', table_z, spectrum, precision=highest)
    spectrum = spectrum * (fx_resp[:, None, None] * fy_resp[None, :, None] * fz_resp[None, None, :])
    spectrum = jnp.einsum('ia,abc->ibc', table_x, spectrum, precision=highest)
    spectrum = jnp.einsum('jb,ibc->ijc', table_y, spectrum, precision=highest)
    spectrum = jnp.einsum('kc,ijc->ijk', table_z, spectrum, precision=highest)
    factor = 2.0 / (NX + 1) * (2.0 / (NY + 1)) * (2.0 / (NZ + 1))
    smooth_gradient = spectrum * (factor * spread_scale(fx_resp, fy_resp, fz_resp))
    return (raw_gradient, smooth_gradient)
```

```python
import math

import jax
import jax.numpy as jnp
import numpy as np
from jax import lax
from jax.experimental import pallas as pl
from jax.experimental.pallas import tpu as pltpu
from jax.sharding import PartitionSpec as P

SMOOTH_X = 32
SMOOTH_YZ = 4
COEFS = (8.0 / 5.0, -1.0 / 5.0, 8.0 / 315.0, -1.0 / 560.0)
CENTER = -205.0 / 72.0
REACH = 4
HIGHEST = lax.Precision.HIGHEST
MESH = pl.DeviceIdType.MESH

SCALE = 5040.0
WHOLE = tuple(float(round(SCALE * weight)) for weight in COEFS)
MIDDLE = 3.0 * float(round(SCALE * CENTER))

VMEM = pl.BlockSpec(memory_space=pltpu.VMEM)
SMEM = pl.BlockSpec(memory_space=pltpu.SMEM)
HBM = pl.BlockSpec(memory_space=pltpu.HBM)


def smoothing_table(length, strength):
    counter = np.arange(1, length + 1, dtype=np.float64)
    sines = np.sin(np.pi * np.outer(counter, counter) / (length + 1))
    half_sine = np.sin(np.pi * counter / (2 * (length + 1)))
    resp = 1.0 / (1.0 + strength * 4.0 * half_sine**2)
    table = 2.0 / (length + 1) * (sines * resp[None, :]) @ sines
    return table, 1.0 / math.sqrt(np.mean(resp * resp))


def stencil_tables(width_y, width_z):
    def bands(length):
        return sum(
            weight * (np.eye(length, k=offset + 1) + np.eye(length, k=-offset - 1))
            for offset, weight in enumerate(WHOLE)
        )

    band_y = bands(width_y)
    band_z = np.kron(np.eye(2), bands(width_z))
    return (
        jnp.asarray(np.concatenate([band_y, band_y], axis=1), jnp.bfloat16),
        jnp.asarray(np.concatenate([band_z, band_z], axis=0), jnp.bfloat16),
    )


def split(cell, width):
    if width & (width - 1) == 0:
        return cell >> (width.bit_length() - 1), cell & (width - 1)
    return lax.div(cell, width), lax.rem(cell, width)


def inject_kernel(
    rec_cell, rec_data, src_cell, src_sign, wavelet, late, now,
    late_out, now_out, first_out, second_out, picks, sems,
):
    size = late_out.shape[0] * late_out.shape[1]
    width = late_out.shape[1]
    first = lax.axis_index("mp") * size
    copies = [
        pltpu.make_async_copy(late, late_out, sems.at[0]),
        pltpu.make_async_copy(now, now_out, sems.at[1]),
    ]
    for copy in copies:
        copy.start()
    rows = late_out.shape[0]
    step = math.gcd(rows, 64)

    def clear(index, carry):
        place = pl.ds(pl.multiple_of(index * step, step), step)
        zero = jnp.zeros((step, width), jnp.float32)
        first_out[place, :] = zero
        second_out[place, :] = zero
        return carry

    lax.fori_loop(0, rows // step, clear, 0)
    lanes = lax.broadcasted_iota(jnp.int32, (1, width), 1)

    def choose(cells):
        total = cells.shape[-1]
        together = math.gcd(total, 16)

        def some(index, count):
            for extra in range(together):
                item = index * together + extra
                local = cells[0, item] - first
                picks[count] = item
                count += jnp.where((local >= 0) & (local < size), 1, 0)
            return count

        return lax.fori_loop(0, total // together, some, 0)

    def add(cells, values, outs):
        count = choose(cells)
        group = 4

        def some(index, carry):
            places, masks, added = [], [], [[] for _ in outs]
            for extra in range(group):
                at = index * group + extra
                live = at < count
                item = jnp.where(live, picks[at], 0)
                place, lane = split(jnp.where(live, cells[0, item] - first, 0), width)
                places.append(place)
                mask = lanes == jnp.where(live, lane, -1)
                for side, value in enumerate(values(item)):
                    added[side].append(jnp.where(mask, value, 0.0))
            for side, out in enumerate(outs):
                sums = []
                for later in range(group):
                    total = added[side][later]
                    for early in range(later):
                        total += jnp.where(places[early] == places[later], added[side][early], 0.0)
                    sums.append(out[pl.ds(places[later], 1), :] + total)
                for place, total in zip(places, sums):
                    out[pl.ds(place, 1), :] = total
            return carry

        lax.fori_loop(0, lax.div(count + (group - 1), group), some, 0)

    def source_values(item):
        sign = (2 * src_sign[0, item] - 1).astype(jnp.float32)
        return sign * wavelet[0, 0, item], sign * wavelet[0, 1, item]

    add(src_cell, source_values, (first_out, second_out))
    for copy in copies:
        copy.wait()
    add(rec_cell, lambda item: (-rec_data[0, 0, item], -rec_data[0, 1, item]), (late_out, now_out))


def inject(rec_cell, rec_data, src_cell, src_sign, wavelet, late, now):
    shape = jax.ShapeDtypeStruct(late.shape, jnp.float32)
    most = max(rec_cell.shape[-1], src_cell.shape[-1])
    return pl.pallas_call(
        inject_kernel,
        out_shape=(shape,) * 4,
        in_specs=[SMEM] * 5 + [HBM] * 2,
        out_specs=(VMEM,) * 4,
        scratch_shapes=[pltpu.SMEM((most + 8,), jnp.int32), pltpu.SemaphoreType.DMA((2,))],
        compiler_params=pltpu.CompilerParams(vmem_limit_bytes=20 * 2**20),
        name="inject",
    )(rec_cell, rec_data, src_cell, src_sign, wavelet, late, now)


def slab_tables(table, count, order):
    rows = table.shape[0] // count
    mixes, sums = [], []
    for me in range(count):
        own = slice(me * rows, (me + 1) * rows)
        sums.append(np.stack([table[me * rows, own][order], table[(me + 1) * rows - 1, own][order]]))
        columns = [table[own, own][:, order]]
        for shift in range(1, count):
            source = (me - shift) % count
            seen = (source + 1) * rows - 1 if source < me else source * rows
            columns.append((table[own, seen] / table[seen, seen])[:, None])
        mixes.append(np.concatenate(columns, axis=1))
    return (
        jnp.asarray(np.stack(mixes).reshape(-1), jnp.float32),
        jnp.asarray(np.stack(sums).reshape(-1), jnp.float32),
    )


def make_kernel(slabs, groups, rows, width_y, width_z):
    blocks = rows // REACH
    chips = groups // 2
    lines = width_y // groups
    lanes = max(lines, min(128, REACH * lines))
    group = lanes // lines
    ratio = slabs // groups
    deep = width_z // slabs
    parts = ((rows - 2 * REACH) // group, 2 * REACH // group)
    starts = (0, parts[0])
    total_places = sum(parts)
    total_rows = ratio * rows
    ready_planes = slabs * total_places * deep * lanes // (width_y * width_z)

    def kernel(
        f_hbm, a_hbm, old_hbm, courant_hbm, late, now, first_source, second_source,
        table_y, table_z, smooth_y, smooth_z, mix, sums,
        raw, smooth,
        fbuf, abuf, obuf, cbuf, nbuf, mbuf, halo_one, halo_two,
        pair_in, chip_in, arrived, spread, lined, planes, planes_in,
        load_sem, one_send, one_recv, two_send, two_recv, pair_send, pair_recv,
        chip_send, chip_recv, turn_send, turn_recv, plane_send, plane_recv,
    ):
        m, s = lax.axis_index("mp"), lax.axis_index("shot")
        core = lax.rem(s, 2)
        chip = lax.div(s, 2)
        exists = (m > 0, m < slabs - 1)
        beside = (m - 1, m + 1)
        partner = s + 1 - 2 * core

        barrier = pltpu.get_barrier_semaphore()
        peers = slabs * groups
        me = m * groups + s

        def greet(index, carry):
            other = lax.rem(me + index, peers)
            pl.semaphore_signal(
                barrier, inc=1,
                device_id={"mp": lax.div(other, groups), "shot": lax.rem(other, groups)},
                device_id_type=MESH,
            )
            return carry

        lax.fori_loop(1, peers, greet, 0)

        term = abuf.reshape(rows + 2 * REACH, chips, 2, lines, width_z)
        pair = fbuf.at[: rows // 2].reshape(rows, chips, lines, width_z)
        ready = fbuf.at[rows // 2 : rows // 2 + ready_planes].reshape(slabs, total_places, deep, lanes)
        buffers = ((f_hbm, fbuf, REACH), (a_hbm, abuf, REACH), (old_hbm, obuf, 0), (courant_hbm, cbuf, 0))

        def load(which, block):
            source, target, pad = buffers[which]
            return pltpu.make_async_copy(
                source.at[pl.ds(block * REACH, REACH)],
                target.at[pl.ds(block * REACH + pad, REACH)],
                load_sem.at[which, block],
            )

        for block in range(blocks):
            for which in range(4):
                load(which, block).start()
        for buf in (fbuf, abuf, nbuf, mbuf):
            zero = jnp.zeros((REACH,) + buf.shape[1:], jnp.float32)
            buf[:REACH] = zero
            buf[REACH + rows :] = zero

        pl.semaphore_wait(barrier, peers - 1)

        def one_copy(side, field, reach):
            row = reach if side == 0 else rows - 1 - reach
            return pltpu.make_async_remote_copy(
                src_ref=(f_hbm, a_hbm)[field].at[row],
                dst_ref=halo_one.at[1 - side, field, reach],
                send_sem=one_send.at[side, field, reach],
                recv_sem=one_recv.at[1 - side, field, reach],
                device_id={"mp": beside[side]},
                device_id_type=MESH,
            )

        def two_copy(side, field, reach):
            row = reach if side == 0 else rows - 1 - reach
            return pltpu.make_async_remote_copy(
                src_ref=(nbuf, mbuf)[field].at[REACH + row],
                dst_ref=halo_two.at[1 - side, field, reach],
                send_sem=two_send.at[side, field, reach],
                recv_sem=two_recv.at[1 - side, field, reach],
                device_id={"mp": beside[side]},
                device_id_type=MESH,
            )

        def landed(buffer, sem, side, field, reach):
            ref = buffer.at[side, field, reach]
            return pltpu.make_async_copy(ref, ref, sem.at[side, field, reach])

        for side in range(2):

            @pl.when(exists[side])
            def _():
                for reach in range(REACH):
                    for field in range(2):
                        one_copy(side, field, reach).start()

        spread[...] = jnp.zeros(spread.shape, jnp.float32)
        for source in range(groups):
            for part in range(group):
                top = source * lanes + part * lines
                spread[top : top + lines, part * width_y : (part + 1) * width_y] = smooth_y[
                    source * lines : (source + 1) * lines, :
                ]

        def laplace(place, fields):
            centers = [field[place] for field in fields]
            both = jnp.concatenate(centers, axis=1)
            high = both.astype(jnp.bfloat16)
            low = (both - high.astype(jnp.float32)).astype(jnp.bfloat16)
            total = jnp.dot(
                table_y[...], jnp.concatenate([high, low], axis=0), preferred_element_type=jnp.float32
            ) + jnp.dot(
                jnp.concatenate([high, low], axis=1), table_z[...], preferred_element_type=jnp.float32
            )
            laps = []
            for side, field in enumerate(fields):
                lap = total[:, side * width_z : (side + 1) * width_z] + MIDDLE * centers[side]
                for offset, weight in enumerate(WHOLE):
                    lap += weight * (field[place + offset + 1] + field[place - offset - 1])
                laps.append(lap)
            return centers, laps

        def plane(flat, row):
            return flat[pl.ds(pl.multiple_of(row * width_y, width_y), width_y), :]

        def first_block(block, carry):
            @pl.when(block + 1 < blocks)
            def _():
                for which in range(4):
                    load(which, block + 1).wait()

            for extra in range(REACH):
                row = block * REACH + extra
                (f_row, a_row), (lap_f, lap_a) = laplace(row + REACH, (fbuf, abuf))
                here = cbuf[row] * (1.0 / SCALE)
                accel = here * lap_f + plane(first_source, row)
                nbuf[row + REACH] = (2.0 * f_row - obuf[row]) + accel
                obuf[row] = accel
                mbuf[row + REACH] = (2.0 * a_row - plane(late, row)) + here * lap_a
            return carry

        for which in range(4):
            load(which, 0).wait()
        lax.fori_loop(0, blocks, first_block, 0)

        def first_edge(reach):
            for side in range(2):

                @pl.when(exists[side])
                def _():
                    for field in range(2):
                        landed(halo_one, one_recv, side, field, reach).wait()
                    for near in range(REACH - reach):
                        row = near if side == 0 else rows - 1 - near
                        here = COEFS[reach + near] * cbuf[row]
                        add_f = here * halo_one[side, 0, reach]
                        obuf[row] += add_f
                        nbuf[row + REACH] += add_f
                        mbuf[row + REACH] += here * halo_one[side, 1, reach]
                    for field in range(2):
                        two_copy(side, field, REACH - 1 - reach).start()

        def second_block(block):
            for extra in range(REACH):
                row = block * REACH + extra
                (_, a_row), (lap_f, lap_a) = laplace(row + REACH, (nbuf, mbuf))
                here = cbuf[row] * (1.0 / SCALE)
                accel_second = here * lap_f + plane(second_source, row)
                a_first = (2.0 * a_row - plane(now, row)) + here * lap_a
                value = a_first * obuf[row] + a_row * accel_second
                term[row] = value.reshape(chips, 2, lines, width_z)

        def pair_copy(block):
            return pltpu.make_async_remote_copy(
                src_ref=term.at[pl.ds(block * REACH, REACH), :, 1 - core],
                dst_ref=pair_in.at[pl.ds(block * REACH, REACH)],
                send_sem=pair_send.at[block],
                recv_sem=pair_recv.at[block],
                device_id={"shot": partner},
                device_id_type=MESH,
            )

        def chip_copy(shift, block):
            other = lax.rem(chip + shift, chips)
            return pltpu.make_async_remote_copy(
                src_ref=pair.at[pl.ds(block * REACH, REACH), other],
                dst_ref=chip_in.at[shift - 1, pl.ds(block * REACH, REACH)],
                send_sem=chip_send.at[shift - 1, block],
                recv_sem=chip_recv.at[shift - 1, block],
                device_id={"shot": other * 2 + core},
                device_id_type=MESH,
            )

        def add_pair(block):
            pair_copy(block).wait_recv()
            here = pl.ds(block * REACH, REACH)
            pair[here] = term[here, :, core] + pair_in[here]
            for shift in range(1, chips):
                chip_copy(shift, block).start()

        def add_chips(block):
            here = pl.ds(block * REACH, REACH)
            value = pair[here, chip]
            for shift in range(1, chips):
                chip_copy(shift, block).wait_recv()
                value += chip_in[shift - 1, here]
            raw[here] = value / float(groups)

        def turn_rows(start, count, place):
            turned = lax.dot_general(
                smooth_z[...],
                raw[start : start + count].reshape(count * lines, width_z),
                (((1,), (1,)), ((), ())),
                precision=HIGHEST,
                preferred_element_type=jnp.float32,
            )
            for index in range(count // group):
                for target in range(slabs):
                    ready[target, place + index] = turned[
                        target * deep : (target + 1) * deep, index * lanes : (index + 1) * lanes
                    ]

        goal = lax.div(m, ratio)
        slot = lax.rem(m, ratio) * groups + s

        def turn_copy(part, shift):
            target = lax.rem(m + shift, slabs)
            place = pl.ds(starts[part], parts[part])
            return pltpu.make_async_remote_copy(
                src_ref=ready.at[target, place],
                dst_ref=arrived.at[slot, place],
                send_sem=turn_send.at[part, target],
                recv_sem=turn_recv.at[part, slot],
                device_id={"mp": target, "shot": goal},
                device_id_type=MESH,
            )

        def turn_start(part):
            for shift in range(1, slabs):
                turn_copy(part, shift).start()

            @pl.when(s != goal)
            def _():
                turn_copy(part, 0).start()

            @pl.when(s == goal)
            def _():
                place = pl.ds(starts[part], parts[part])
                pltpu.make_async_copy(
                    ready.at[m, place], arrived.at[slot, place], turn_recv.at[part, slot]
                ).start()

        def turn_wait(part):
            place = pl.ds(starts[part], parts[part])
            for index in range(ratio * groups):
                ref = arrived.at[index, place]
                pltpu.make_async_copy(ref, ref, turn_recv.at[part, index]).wait()

        inner = list(range(2, blocks - 2))
        near = [block for block in (1, blocks - 2) if 0 < block < blocks - 1]
        near = sorted(set(near) - set(inner))
        edges = [0, blocks - 1]

        first_edge(0)
        first_edge(1)
        for block in inner:
            second_block(block)
            pair_copy(block).start()
        first_edge(2)
        for block in inner:
            add_pair(block)
        first_edge(3)
        for block in near:
            second_block(block)
            pair_copy(block).start()
        for block in edges:
            second_block(block)
        for block in near:
            add_pair(block)
        for block in inner + near:
            add_chips(block)
        turn_rows(REACH, rows - 2 * REACH, 0)

        for reach in reversed(range(REACH)):
            for side in range(2):

                @pl.when(exists[side])
                def _():
                    for field in range(2):
                        landed(halo_two, two_recv, side, field, reach).wait()
                    for close in range(REACH - reach):
                        row = close if side == 0 else rows - 1 - close
                        here = COEFS[reach + close] * cbuf[row]
                        extra = halo_two[side, 1, reach] * obuf[row] + mbuf[row + REACH] * halo_two[side, 0, reach]
                        term[row] += (here * extra).reshape(chips, 2, lines, width_z)

        for block in edges:
            pair_copy(block).start()
        turn_start(0)
        for block in edges:
            add_pair(block)
        for block in edges:
            add_chips(block)
        turn_rows(0, REACH, parts[0])
        turn_rows(rows - REACH, REACH, parts[0] + REACH // group)
        turn_start(1)

        turn_wait(0)
        turn_wait(1)
        for index in range(ratio):
            joined = jnp.concatenate(
                [
                    arrived[index * groups + source].reshape(total_places * deep, lanes)
                    for source in range(groups)
                ],
                axis=1,
            )
            done = jnp.dot(joined, spread[...], precision=HIGHEST, preferred_element_type=jnp.float32)
            for place in range(total_places):
                for part in range(group):
                    lined[(index * total_places + place) * group + part] = done[
                        place * deep : (place + 1) * deep, part * width_y : (part + 1) * width_y
                    ]
        base = s * (2 * total_rows)
        for side in range(2):
            sum_side = sums[base + side * total_rows] * lined[0]
            for row in range(1, total_rows):
                sum_side += sums[base + side * total_rows + row] * lined[row]
            planes[side] = sum_side

        def plane_copy(shift):
            upward = jnp.where(s + shift < groups, 1, 0)
            return pltpu.make_async_remote_copy(
                src_ref=planes.at[upward],
                dst_ref=planes_in.at[shift - 1],
                send_sem=plane_send.at[shift - 1],
                recv_sem=plane_recv.at[shift - 1],
                device_id={"shot": lax.rem(s + shift, groups)},
                device_id_type=MESH,
            )

        for shift in range(1, groups):
            plane_copy(shift).start()
        for shift in range(1, groups):
            plane_copy(shift).wait_recv()
        wide = total_rows + groups - 1
        step = math.gcd(total_rows, 4)

        def mixed(index, carry):
            start = index * step
            totals = [None] * step
            for source in range(wide):
                value = lined[source] if source < total_rows else planes_in[source - total_rows]
                for extra in range(step):
                    piece = mix[(s * total_rows + start + extra) * wide + source] * value
                    totals[extra] = piece if source == 0 else totals[extra] + piece
            for extra in range(step):
                smooth[start + extra] = totals[extra]
            return carry

        lax.fori_loop(0, total_rows // step, mixed, 0)

        for side in range(2):

            @pl.when(exists[side])
            def _():
                for reach in range(REACH):
                    for field in range(2):
                        one_copy(side, field, reach).wait_send()
                        two_copy(side, field, reach).wait_send()

        for block in range(blocks):
            pair_copy(block).wait_send()
            for shift in range(1, chips):
                chip_copy(shift, block).wait_send()
        for part in range(2):
            for shift in range(1, slabs):
                turn_copy(part, shift).wait_send()

            @pl.when(s != goal)
            def _():
                turn_copy(part, 0).wait_send()

        for shift in range(1, groups):
            plane_copy(shift).wait_send()

    padded = pltpu.VMEM((rows + 2 * REACH, width_y, width_z), jnp.float32)
    slab = pltpu.VMEM((rows, width_y, width_z), jnp.float32)
    halo = pltpu.VMEM((2, 2, REACH, width_y, width_z), jnp.float32)
    dma = pltpu.SemaphoreType.DMA
    scratch = [
        padded, padded, slab, slab, padded, padded,
        halo, halo,
        pltpu.VMEM((rows, chips, lines, width_z), jnp.float32),
        pltpu.VMEM((max(1, chips - 1), rows, lines, width_z), jnp.float32),
        pltpu.VMEM((ratio * groups, total_places, deep, lanes), jnp.float32),
        pltpu.VMEM((groups * lanes, group * width_y), jnp.float32),
        pltpu.VMEM((total_rows, deep, width_y), jnp.float32),
        pltpu.VMEM((2, deep, width_y), jnp.float32),
        pltpu.VMEM((max(1, groups - 1), deep, width_y), jnp.float32),
        dma((4, blocks)),
        dma((2, 2, REACH)), dma((2, 2, REACH)), dma((2, 2, REACH)), dma((2, 2, REACH)),
        dma((blocks,)), dma((blocks,)),
        dma((max(1, chips - 1), blocks)), dma((max(1, chips - 1), blocks)),
        dma((2, slabs)), dma((2, ratio * groups)),
        dma((groups - 1,)), dma((groups - 1,)),
    ]
    outs = (
        jax.ShapeDtypeStruct((rows, lines, width_z), jnp.float32),
        jax.ShapeDtypeStruct((total_rows, deep, width_y), jnp.float32),
    )
    inner_rows = list(range(REACH, rows - REACH)) + list(range(REACH)) + list(range(rows - REACH, rows))
    order = np.concatenate([index * rows + np.array(inner_rows) for index in range(ratio)])
    return kernel, scratch, outs, order


def per_device(
    courant, forward_old, forward_now, adjoint_late, adjoint_now,
    src_cell, src_sign, wavelet, rec_cell, rec_data,
):
    rows, width_y, width_z = courant.shape
    slabs, groups = lax.axis_size("mp"), lax.axis_size("shot")
    flat = (rows * width_y, width_z)
    injected = inject(
        rec_cell.reshape(1, -1), rec_data, src_cell, src_sign, wavelet,
        adjoint_late.reshape(flat), adjoint_now.reshape(flat),
    )
    kernel, scratch, outs, order = make_kernel(slabs, groups, rows, width_y, width_z)
    table_x, spread_x = smoothing_table(rows * slabs, SMOOTH_X**2)
    smooth_y, spread_y = smoothing_table(width_y, SMOOTH_YZ**2)
    smooth_z, spread_z = smoothing_table(width_z, SMOOTH_YZ**2)
    smooth_y = smooth_y * (spread_x * spread_y * spread_z)
    raw, smooth = pl.pallas_call(
        kernel,
        out_shape=outs,
        in_specs=[HBM] * 4 + [VMEM] * 8 + [SMEM] * 2,
        out_specs=(VMEM, VMEM),
        scratch_shapes=scratch,
        compiler_params=pltpu.CompilerParams(
            collective_id=0, has_side_effects=True, vmem_limit_bytes=VMEM_GRANT
        ),
        name="gradient",
    )(
        forward_now[0], adjoint_now[0], forward_old[0], courant, *injected,
        *stencil_tables(width_y, width_z),
        jnp.asarray(smooth_y, jnp.float32), jnp.asarray(smooth_z, jnp.float32),
        *slab_tables(table_x, groups, order),
    )
    return raw, jnp.swapaxes(smooth, 1, 2)


VMEM_GRANT = 50 * 2**20


def solution(mesh):
    step = jax.shard_map(
        per_device,
        mesh=mesh,
        in_specs=(
            P(("parts", "mp"), None, None),
            P(("parts", "shot"), "mp", None, None),
            P(("parts", "shot"), "mp", None, None),
            P(("parts", "shot"), "mp", None, None),
            P(("parts", "shot"), "mp", None, None),
            P(("parts", "shot"), None),
            P(("parts", "shot"), None),
            P(("parts", "shot"), None, None),
            P("parts"),
            P(("parts", "shot"), None, None),
        ),
        out_specs=(P(("parts", "mp"), "shot", None), P(("parts", "shot"), None, "mp")),
        check_vma=False,
    )
    return step
```

```python
import math

import jax
import jax.numpy as jnp
import numpy as np
from jax import lax
from jax.experimental import pallas as pl
from jax.experimental.pallas import tpu as pltpu
from jax.sharding import PartitionSpec as P

SMOOTH_X = 32
SMOOTH_YZ = 4
COEFS = (8.0 / 5.0, -1.0 / 5.0, 8.0 / 315.0, -1.0 / 560.0)
CENTER = -205.0 / 72.0
REACH = 4
HIGHEST = lax.Precision.HIGHEST
MESH = pl.DeviceIdType.MESH

SCALE = 5040.0
WHOLE = tuple(float(round(SCALE * weight)) for weight in COEFS)
MIDDLE = 3.0 * float(round(SCALE * CENTER))

VMEM = pl.BlockSpec(memory_space=pltpu.VMEM)
SMEM = pl.BlockSpec(memory_space=pltpu.SMEM)
HBM = pl.BlockSpec(memory_space=pltpu.HBM)


def smoothing_table(length, strength):
    counter = np.arange(1, length + 1, dtype=np.float64)
    sines = np.sin(np.pi * np.outer(counter, counter) / (length + 1))
    half_sine = np.sin(np.pi * counter / (2 * (length + 1)))
    resp = 1.0 / (1.0 + strength * 4.0 * half_sine**2)
    table = 2.0 / (length + 1) * (sines * resp[None, :]) @ sines
    return table, 1.0 / math.sqrt(np.mean(resp * resp))


def stencil_tables(width_y, width_z):
    def bands(length):
        return sum(
            weight * (np.eye(length, k=offset + 1) + np.eye(length, k=-offset - 1))
            for offset, weight in enumerate(WHOLE)
        )

    band_y = bands(width_y)
    band_z = np.kron(np.eye(2), bands(width_z))
    return (
        jnp.asarray(np.concatenate([band_y, band_y], axis=1), jnp.bfloat16),
        jnp.asarray(np.concatenate([band_z, band_z], axis=0), jnp.bfloat16),
    )


def split(cell, width):
    if width & (width - 1) == 0:
        return cell >> (width.bit_length() - 1), cell & (width - 1)
    return lax.div(cell, width), lax.rem(cell, width)


def inject_kernel(
    rec_cell, rec_data, src_cell, src_sign, wavelet, late, now,
    late_out, now_out, first_out, second_out,
    late_buf, now_buf, first_buf, second_buf,
    rec_cells, rec_values, src_cells, src_signs, src_values, picks, sems,
):
    rows, width = late_buf.shape
    size = rows * width
    first = lax.axis_index("mp") * size
    moves = [
        (rec_cell, rec_cells), (rec_data, rec_values), (src_cell, src_cells),
        (src_sign, src_signs), (wavelet, src_values), (late, late_buf), (now, now_buf),
        (first_buf, first_out), (second_buf, second_out), (late_buf, late_out), (now_buf, now_out),
    ]
    copies = [
        pltpu.make_async_copy(source, target, sems.at[index])
        for index, (source, target) in enumerate(moves)
    ]
    for copy in copies[:7]:
        copy.start()
    step = math.gcd(rows, 64)

    def clear(index, carry):
        place = pl.ds(pl.multiple_of(index * step, step), step)
        zero = jnp.zeros((step, width), jnp.float32)
        first_buf[place, :] = zero
        second_buf[place, :] = zero
        return carry

    lax.fori_loop(0, rows // step, clear, 0)
    lanes = lax.broadcasted_iota(jnp.int32, (1, width), 1)

    def choose(load, total):
        together = math.gcd(total, 16)

        def some(index, count):
            items = [index * together + extra for extra in range(together)]
            locals_ = [load(item) - first for item in items]
            valid = [jnp.where((local >= 0) & (local < size), 1, 0) for local in locals_]
            for item, ok in zip(items, valid):
                picks[count] = item
                count += ok
            return count

        return lax.fori_loop(0, total // together, some, 0)

    def add(count, load, values, outs):
        group = 4

        def some(index, carry):
            ats = [index * group + extra for extra in range(group)]
            lives = [at < count for at in ats]
            items = [jnp.where(live, picks[at], 0) for at, live in zip(ats, lives)]
            cells = [load(item) - first for item in items]
            amounts = [values(item) for item in items]
            places, added = [], [[] for _ in outs]
            for cell, live, amount in zip(cells, lives, amounts):
                place, lane = split(jnp.where(live, cell, 0), width)
                places.append(place)
                mask = lanes == jnp.where(live, lane, -1)
                for side, value in enumerate(amount):
                    added[side].append(jnp.where(mask, value, 0.0))
            olds = [[out[pl.ds(place, 1), :] for place in places] for out in outs]
            for side, out in enumerate(outs):
                sums = []
                for later in range(group):
                    total = added[side][later]
                    for early in range(later):
                        total += jnp.where(places[early] == places[later], added[side][early], 0.0)
                    sums.append(olds[side][later] + total)
                for place, total in zip(places, sums):
                    out[pl.ds(place, 1), :] = total
            return carry

        lax.fori_loop(0, lax.div(count + (group - 1), group), some, 0)

    def source_values(item):
        sign = (2 * src_signs[0, item] - 1).astype(jnp.float32)
        return sign * src_values[0, 0, item], sign * src_values[0, 1, item]

    for copy in copies[:5]:
        copy.wait()
    count = choose(lambda item: src_cells[0, item], src_cells.shape[1])
    add(count, lambda item: src_cells[0, item], source_values, (first_buf, second_buf))
    copies[7].start()
    copies[8].start()
    count = choose(lambda item: rec_cells[item], rec_cells.shape[0])
    copies[5].wait()
    copies[6].wait()
    add(
        count, lambda item: rec_cells[item],
        lambda item: (-rec_values[0, 0, item], -rec_values[0, 1, item]), (late_buf, now_buf),
    )
    copies[9].start()
    copies[10].start()
    for copy in copies[7:]:
        copy.wait()


def inject(rec_cell, rec_data, src_cell, src_sign, wavelet, late, now):
    shape = jax.ShapeDtypeStruct(late.shape, jnp.float32)
    most = max(rec_cell.shape[-1], src_cell.shape[-1])
    small = (rec_cell, rec_data, src_cell, src_sign, wavelet)
    return pl.pallas_call(
        inject_kernel,
        out_shape=(shape,) * 4,
        in_specs=[HBM] * 7,
        out_specs=(HBM,) * 4,
        scratch_shapes=[pltpu.VMEM(late.shape, jnp.float32)] * 4
        + [pltpu.SMEM(array.shape, array.dtype) for array in small]
        + [pltpu.SMEM((most + 8,), jnp.int32), pltpu.SemaphoreType.DMA((11,))],
        compiler_params=pltpu.CompilerParams(vmem_limit_bytes=VMEM_GRANT),
        name="inject",
    )(*small, late, now)


def slab_tables(table, count, order):
    rows = table.shape[0] // count
    mixes, sums = [], []
    for me in range(count):
        own = slice(me * rows, (me + 1) * rows)
        sums.append(np.stack([table[me * rows, own][order], table[(me + 1) * rows - 1, own][order]]))
        columns = [table[own, own][:, order]]
        for shift in range(1, count):
            source = (me - shift) % count
            seen = (source + 1) * rows - 1 if source < me else source * rows
            columns.append((table[own, seen] / table[seen, seen])[:, None])
        mixes.append(np.concatenate(columns, axis=1))
    return (
        jnp.asarray(np.stack(mixes).reshape(-1), jnp.float32),
        jnp.asarray(np.stack(sums).reshape(-1), jnp.float32),
    )


def make_kernel(slabs, groups, rows, width_y, width_z):
    blocks = rows // REACH
    chips = groups // 2
    lines = width_y // groups
    lanes = max(lines, min(128, REACH * lines))
    group = lanes // lines
    ratio = slabs // groups
    deep = width_z // slabs
    parts = ((rows - 2 * REACH) // group, 2 * REACH // group)
    starts = (0, parts[0])
    total_places = sum(parts)
    total_rows = ratio * rows
    ready_planes = slabs * total_places * deep * lanes // (width_y * width_z)

    def kernel(
        f_hbm, a_hbm, old_hbm, courant_hbm, late_hbm, now_hbm, first_hbm, second_hbm,
        table_y, table_z, smooth_y, smooth_z, sums,
        raw_out, lined, planes_in,
        raw, fbuf, abuf, obuf, cbuf, nbuf, mbuf, lbuf, sbuf, halo_one, halo_two,
        pair_in, chip_in, arrived, spread, planes,
        load_sem, one_send, one_recv, two_send, two_recv, pair_send, pair_recv,
        chip_send, chip_recv, turn_send, turn_recv, plane_send, plane_recv,
    ):
        m, s = lax.axis_index("mp"), lax.axis_index("shot")
        core = lax.rem(s, 2)
        chip = lax.div(s, 2)
        exists = (m > 0, m < slabs - 1)
        beside = (m - 1, m + 1)
        partner = s + 1 - 2 * core

        inner = list(range(2, blocks - 2))
        near = [block for block in (1, blocks - 2) if 0 < block < blocks - 1]
        near = sorted(set(near) - set(inner))
        edges = [0, blocks - 1]

        barrier = pltpu.get_barrier_semaphore()
        peers = slabs * groups
        me = m * groups + s

        def greet(index, carry):
            other = lax.rem(me + index, peers)
            pl.semaphore_signal(
                barrier, inc=1,
                device_id={"mp": lax.div(other, groups), "shot": lax.rem(other, groups)},
                device_id_type=MESH,
            )
            return carry

        lax.fori_loop(1, peers, greet, 0)

        term = abuf.reshape(rows + 2 * REACH, chips, 2, lines, width_z)
        pair = fbuf.at[: rows // 2].reshape(rows, chips, lines, width_z)
        ready = fbuf.at[rows // 2 : rows // 2 + ready_planes].reshape(slabs, total_places, deep, lanes)
        buffers = (
            (f_hbm, fbuf, REACH), (a_hbm, abuf, REACH), (old_hbm, obuf, 0), (courant_hbm, cbuf, 0),
            (late_hbm, lbuf, 0), (first_hbm, sbuf, 0), (now_hbm, lbuf, 0), (second_hbm, sbuf, 0),
        )

        def load(which, block):
            source, target, pad = buffers[which]
            return pltpu.make_async_copy(
                source.at[pl.ds(block * REACH, REACH)],
                target.at[pl.ds(block * REACH + pad, REACH)],
                load_sem.at[which, block],
            )

        for block in range(blocks):
            for which in range(6):
                load(which, block).start()
        for buf in (fbuf, abuf, nbuf, mbuf):
            zero = jnp.zeros((REACH,) + buf.shape[1:], jnp.float32)
            buf[:REACH] = zero
            buf[REACH + rows :] = zero

        pl.semaphore_wait(barrier, peers - 1)

        def one_copy(side, field, reach):
            row = reach if side == 0 else rows - 1 - reach
            return pltpu.make_async_remote_copy(
                src_ref=(f_hbm, a_hbm)[field].at[row],
                dst_ref=halo_one.at[1 - side, field, reach],
                send_sem=one_send.at[side, field, reach],
                recv_sem=one_recv.at[1 - side, field, reach],
                device_id={"mp": beside[side]},
                device_id_type=MESH,
            )

        def two_copy(side, field, reach):
            row = reach if side == 0 else rows - 1 - reach
            return pltpu.make_async_remote_copy(
                src_ref=(nbuf, mbuf)[field].at[REACH + row],
                dst_ref=halo_two.at[1 - side, field, reach],
                send_sem=two_send.at[side, field, reach],
                recv_sem=two_recv.at[1 - side, field, reach],
                device_id={"mp": beside[side]},
                device_id_type=MESH,
            )

        def landed(buffer, sem, side, field, reach):
            ref = buffer.at[side, field, reach]
            return pltpu.make_async_copy(ref, ref, sem.at[side, field, reach])

        for side in range(2):

            @pl.when(exists[side])
            def _():
                for reach in range(REACH):
                    for field in range(2):
                        one_copy(side, field, reach).start()

        spread[...] = jnp.zeros(spread.shape, jnp.float32)
        for source in range(groups):
            for part in range(group):
                top = source * lanes + part * lines
                spread[top : top + lines, part * width_y : (part + 1) * width_y] = smooth_y[
                    source * lines : (source + 1) * lines, :
                ]

        def laplace(place, fields):
            centers = [field[place] for field in fields]
            both = jnp.concatenate(centers, axis=1)
            high = both.astype(jnp.bfloat16)
            low = (both - high.astype(jnp.float32)).astype(jnp.bfloat16)
            total = jnp.dot(
                table_y[...], jnp.concatenate([high, low], axis=0), preferred_element_type=jnp.float32
            ) + jnp.dot(
                jnp.concatenate([high, low], axis=1), table_z[...], preferred_element_type=jnp.float32
            )
            laps = []
            for side, field in enumerate(fields):
                lap = total[:, side * width_z : (side + 1) * width_z] + MIDDLE * centers[side]
                for offset, weight in enumerate(WHOLE):
                    lap += weight * (field[place + offset + 1] + field[place - offset - 1])
                laps.append(lap)
            return centers, laps

        def first_block(block, carry):
            @pl.when(block + 1 < blocks)
            def _():
                for which in range(6):
                    load(which, block + 1).wait()

            for extra in range(REACH):
                row = block * REACH + extra
                (f_row, a_row), (lap_f, lap_a) = laplace(row + REACH, (fbuf, abuf))
                here = cbuf[row] * (1.0 / SCALE)
                accel = here * lap_f + sbuf[row]
                nbuf[row + REACH] = (2.0 * f_row - obuf[row]) + accel
                obuf[row] = accel
                mbuf[row + REACH] = (2.0 * a_row - lbuf[row]) + here * lap_a
            return carry

        for which in range(6):
            load(which, 0).wait()
        lax.fori_loop(0, blocks, first_block, 0)
        for block in inner + near + edges:
            for which in (6, 7):
                load(which, block).start()

        def first_edge(reach):
            for side in range(2):

                @pl.when(exists[side])
                def _():
                    for field in range(2):
                        landed(halo_one, one_recv, side, field, reach).wait()
                    for near in range(REACH - reach):
                        row = near if side == 0 else rows - 1 - near
                        here = COEFS[reach + near] * cbuf[row]
                        add_f = here * halo_one[side, 0, reach]
                        obuf[row] += add_f
                        nbuf[row + REACH] += add_f
                        mbuf[row + REACH] += here * halo_one[side, 1, reach]
                    for field in range(2):
                        two_copy(side, field, REACH - 1 - reach).start()

        def second_block(block):
            for which in (6, 7):
                load(which, block).wait()
            for extra in range(REACH):
                row = block * REACH + extra
                (_, a_row), (lap_f, lap_a) = laplace(row + REACH, (nbuf, mbuf))
                here = cbuf[row] * (1.0 / SCALE)
                accel_second = here * lap_f + sbuf[row]
                a_first = (2.0 * a_row - lbuf[row]) + here * lap_a
                value = a_first * obuf[row] + a_row * accel_second
                term[row] = value.reshape(chips, 2, lines, width_z)

        def pair_copy(block):
            return pltpu.make_async_remote_copy(
                src_ref=term.at[pl.ds(block * REACH, REACH), :, 1 - core],
                dst_ref=pair_in.at[pl.ds(block * REACH, REACH)],
                send_sem=pair_send.at[block],
                recv_sem=pair_recv.at[block],
                device_id={"shot": partner},
                device_id_type=MESH,
            )

        def chip_copy(shift, block):
            other = lax.rem(chip + shift, chips)
            return pltpu.make_async_remote_copy(
                src_ref=pair.at[pl.ds(block * REACH, REACH), other],
                dst_ref=chip_in.at[shift - 1, pl.ds(block * REACH, REACH)],
                send_sem=chip_send.at[shift - 1, block],
                recv_sem=chip_recv.at[shift - 1, block],
                device_id={"shot": other * 2 + core},
                device_id_type=MESH,
            )

        def add_pair(block):
            pair_copy(block).wait_recv()
            here = pl.ds(block * REACH, REACH)
            pair[here] = term[here, :, core] + pair_in[here]
            for shift in range(1, chips):
                chip_copy(shift, block).start()

        def add_chips(block):
            here = pl.ds(block * REACH, REACH)
            value = pair[here, chip]
            for shift in range(1, chips):
                chip_copy(shift, block).wait_recv()
                value += chip_in[shift - 1, here]
            raw[here] = value / float(groups)

        def turn_rows(start, count, place):
            turned = lax.dot_general(
                smooth_z[...],
                raw[start : start + count].reshape(count * lines, width_z),
                (((1,), (1,)), ((), ())),
                precision=HIGHEST,
                preferred_element_type=jnp.float32,
            )
            for index in range(count // group):
                for target in range(slabs):
                    ready[target, place + index] = turned[
                        target * deep : (target + 1) * deep, index * lanes : (index + 1) * lanes
                    ]

        goal = lax.div(m, ratio)
        slot = lax.rem(m, ratio) * groups + s

        def turn_copy(part, shift):
            target = lax.rem(m + shift, slabs)
            place = pl.ds(starts[part], parts[part])
            return pltpu.make_async_remote_copy(
                src_ref=ready.at[target, place],
                dst_ref=arrived.at[slot, place],
                send_sem=turn_send.at[part, target],
                recv_sem=turn_recv.at[part, slot],
                device_id={"mp": target, "shot": goal},
                device_id_type=MESH,
            )

        def turn_start(part):
            for shift in range(1, slabs):
                turn_copy(part, shift).start()

            @pl.when(s != goal)
            def _():
                turn_copy(part, 0).start()

            @pl.when(s == goal)
            def _():
                place = pl.ds(starts[part], parts[part])
                pltpu.make_async_copy(
                    ready.at[m, place], arrived.at[slot, place], turn_recv.at[part, slot]
                ).start()

        def turn_wait(part):
            place = pl.ds(starts[part], parts[part])
            for index in range(ratio * groups):
                ref = arrived.at[index, place]
                pltpu.make_async_copy(ref, ref, turn_recv.at[part, index]).wait()

        first_edge(0)
        first_edge(1)
        for block in inner:
            second_block(block)
            pair_copy(block).start()
        first_edge(2)
        for block in inner:
            add_pair(block)
        first_edge(3)
        for block in near:
            second_block(block)
            pair_copy(block).start()
        for block in edges:
            second_block(block)
        for block in near:
            add_pair(block)
        for block in inner + near:
            add_chips(block)
        turn_rows(REACH, rows - 2 * REACH, 0)

        for reach in reversed(range(REACH)):
            for side in range(2):

                @pl.when(exists[side])
                def _():
                    for field in range(2):
                        landed(halo_two, two_recv, side, field, reach).wait()
                    for close in range(REACH - reach):
                        row = close if side == 0 else rows - 1 - close
                        here = COEFS[reach + close] * cbuf[row]
                        extra = halo_two[side, 1, reach] * obuf[row] + mbuf[row + REACH] * halo_two[side, 0, reach]
                        term[row] += (here * extra).reshape(chips, 2, lines, width_z)

        for block in edges:
            pair_copy(block).start()
        turn_start(0)
        for block in edges:
            add_pair(block)
        for block in edges:
            add_chips(block)
        turn_rows(0, REACH, parts[0])
        turn_rows(rows - REACH, REACH, parts[0] + REACH // group)
        turn_start(1)
        raw_copy = pltpu.make_async_copy(raw, raw_out, load_sem.at[0, 0])
        raw_copy.start()

        turn_wait(0)
        turn_wait(1)
        for index in range(ratio):
            joined = jnp.concatenate(
                [
                    arrived[index * groups + source].reshape(total_places * deep, lanes)
                    for source in range(groups)
                ],
                axis=1,
            )
            done = jnp.dot(joined, spread[...], precision=HIGHEST, preferred_element_type=jnp.float32)
            for place in range(total_places):
                for part in range(group):
                    lined[(index * total_places + place) * group + part] = done[
                        place * deep : (place + 1) * deep, part * width_y : (part + 1) * width_y
                    ]
        base = s * (2 * total_rows)
        for side in range(2):
            sum_side = sums[base + side * total_rows] * lined[0]
            for row in range(1, total_rows):
                sum_side += sums[base + side * total_rows + row] * lined[row]
            planes[side] = sum_side

        def plane_copy(shift):
            upward = jnp.where(s + shift < groups, 1, 0)
            return pltpu.make_async_remote_copy(
                src_ref=planes.at[upward],
                dst_ref=planes_in.at[shift - 1],
                send_sem=plane_send.at[shift - 1],
                recv_sem=plane_recv.at[shift - 1],
                device_id={"shot": lax.rem(s + shift, groups)},
                device_id_type=MESH,
            )

        for shift in range(1, groups):
            plane_copy(shift).start()
        for shift in range(1, groups):
            plane_copy(shift).wait_recv()
        for side in range(2):

            @pl.when(exists[side])
            def _():
                for reach in range(REACH):
                    for field in range(2):
                        one_copy(side, field, reach).wait_send()
                        two_copy(side, field, reach).wait_send()

        for block in range(blocks):
            pair_copy(block).wait_send()
            for shift in range(1, chips):
                chip_copy(shift, block).wait_send()
        for part in range(2):
            for shift in range(1, slabs):
                turn_copy(part, shift).wait_send()

            @pl.when(s != goal)
            def _():
                turn_copy(part, 0).wait_send()

        for shift in range(1, groups):
            plane_copy(shift).wait_send()
        raw_copy.wait()

    padded = pltpu.VMEM((rows + 2 * REACH, width_y, width_z), jnp.float32)
    slab = pltpu.VMEM((rows, width_y, width_z), jnp.float32)
    halo = pltpu.VMEM((2, 2, REACH, width_y, width_z), jnp.float32)
    dma = pltpu.SemaphoreType.DMA
    scratch = [
        pltpu.VMEM((rows, lines, width_z), jnp.float32),
        padded, padded, slab, slab, padded, padded, slab, slab,
        halo, halo,
        pltpu.VMEM((rows, chips, lines, width_z), jnp.float32),
        pltpu.VMEM((max(1, chips - 1), rows, lines, width_z), jnp.float32),
        pltpu.VMEM((ratio * groups, total_places, deep, lanes), jnp.float32),
        pltpu.VMEM((groups * lanes, group * width_y), jnp.float32),
        pltpu.VMEM((2, deep, width_y), jnp.float32),
        dma((8, blocks)),
        dma((2, 2, REACH)), dma((2, 2, REACH)), dma((2, 2, REACH)), dma((2, 2, REACH)),
        dma((blocks,)), dma((blocks,)),
        dma((max(1, chips - 1), blocks)), dma((max(1, chips - 1), blocks)),
        dma((2, slabs)), dma((2, ratio * groups)),
        dma((groups - 1,)), dma((groups - 1,)),
    ]
    outs = (
        jax.ShapeDtypeStruct((rows, lines, width_z), jnp.float32),
        jax.ShapeDtypeStruct((total_rows, deep, width_y), jnp.float32),
        jax.ShapeDtypeStruct((groups - 1, deep, width_y), jnp.float32),
    )
    inner_rows = list(range(REACH, rows - REACH)) + list(range(REACH)) + list(range(rows - REACH, rows))
    order = np.concatenate([index * rows + np.array(inner_rows) for index in range(ratio)])
    return kernel, scratch, outs, order


def mix_kernel(
    raw_hbm, lined_hbm, planes_hbm, mix, raw_out, smooth, raw, lined, planes, buffer, sems
):
    total_rows, others = lined.shape[0], planes.shape[0]
    wide = total_rows + others
    step = math.gcd(total_rows, 4)
    base = lax.axis_index("shot") * total_rows
    copies = [
        pltpu.make_async_copy(source, target, sems.at[index])
        for index, (source, target) in enumerate(
            [(lined_hbm, lined), (planes_hbm, planes), (raw_hbm, raw), (raw, raw_out)]
        )
    ]
    for copy in copies[:3]:
        copy.start()
    for copy in copies[:3]:
        copy.wait()
    copies[3].start()

    def write(index):
        here = pl.ds(index * step, step)
        return pltpu.make_async_copy(buffer.at[here], smooth.at[here], sems.at[index + 4])

    def some(index, carry):
        totals = [None] * step
        for source in range(wide):
            value = lined[source] if source < total_rows else planes[source - total_rows]
            for extra in range(step):
                piece = mix[(base + index * step + extra) * wide + source] * value
                totals[extra] = piece if source == 0 else totals[extra] + piece
        for extra in range(step):
            buffer[index * step + extra] = totals[extra]
        write(index).start()
        return carry

    lax.fori_loop(0, total_rows // step, some, 0)
    for index in range(total_rows // step):
        write(index).wait()
    copies[3].wait()


def mix_planes(raw, lined, planes, mix):
    steps = lined.shape[0] // math.gcd(lined.shape[0], 4)
    return pl.pallas_call(
        mix_kernel,
        out_shape=(
            jax.ShapeDtypeStruct(raw.shape, jnp.float32),
            jax.ShapeDtypeStruct(lined.shape, jnp.float32),
        ),
        in_specs=[HBM, HBM, HBM, SMEM],
        out_specs=(HBM, HBM),
        scratch_shapes=[
            pltpu.VMEM(raw.shape, jnp.float32), pltpu.VMEM(lined.shape, jnp.float32),
            pltpu.VMEM(planes.shape, jnp.float32), pltpu.VMEM(lined.shape, jnp.float32),
            pltpu.SemaphoreType.DMA((steps + 4,)),
        ],
        compiler_params=pltpu.CompilerParams(vmem_limit_bytes=VMEM_GRANT),
        name="mix",
    )(raw, lined, planes, mix)


def per_device(
    courant, forward_old, forward_now, adjoint_late, adjoint_now,
    src_cell, src_sign, wavelet, rec_cell, rec_data,
):
    rows, width_y, width_z = courant.shape
    slabs, groups = lax.axis_size("mp"), lax.axis_size("shot")
    flat = (rows * width_y, width_z)
    injected = inject(
        rec_cell, rec_data, src_cell, src_sign, wavelet,
        adjoint_late.reshape(flat), adjoint_now.reshape(flat),
    )
    kernel, scratch, outs, order = make_kernel(slabs, groups, rows, width_y, width_z)
    table_x, spread_x = smoothing_table(rows * slabs, SMOOTH_X**2)
    smooth_y, spread_y = smoothing_table(width_y, SMOOTH_YZ**2)
    smooth_z, spread_z = smoothing_table(width_z, SMOOTH_YZ**2)
    smooth_y = smooth_y * (spread_x * spread_y * spread_z)
    mix, sums = slab_tables(table_x, groups, order)
    raw, lined, planes = pl.pallas_call(
        kernel,
        out_shape=outs,
        in_specs=[HBM] * 8 + [VMEM] * 4 + [SMEM],
        out_specs=(HBM, VMEM, VMEM),
        scratch_shapes=scratch,
        compiler_params=pltpu.CompilerParams(
            collective_id=0, has_side_effects=True, vmem_limit_bytes=GRADIENT_GRANT
        ),
        name="gradient",
    )(
        forward_now[0], adjoint_now[0], forward_old[0], courant,
        *(array.reshape(rows, width_y, width_z) for array in injected),
        *stencil_tables(width_y, width_z),
        jnp.asarray(smooth_y, jnp.float32), jnp.asarray(smooth_z, jnp.float32),
        sums,
    )
    raw, smooth = mix_planes(raw, lined, planes, mix)
    return raw, jnp.swapaxes(smooth, 1, 2)


VMEM_GRANT = 60 * 2**20
GRADIENT_GRANT = 56 * 2**20


def solution(mesh):
    step = jax.shard_map(
        per_device,
        mesh=mesh,
        in_specs=(
            P(("parts", "mp"), None, None),
            P(("parts", "shot"), "mp", None, None),
            P(("parts", "shot"), "mp", None, None),
            P(("parts", "shot"), "mp", None, None),
            P(("parts", "shot"), "mp", None, None),
            P(("parts", "shot"), None),
            P(("parts", "shot"), None),
            P(("parts", "shot"), None, None),
            P("parts"),
            P(("parts", "shot"), None, None),
        ),
        out_specs=(P(("parts", "mp"), "shot", None), P(("parts", "shot"), None, "mp")),
        check_vma=False,
    )
    return step
```

```python
import math

import jax
import jax.numpy as jnp
import numpy as np
from jax import lax
from jax.experimental import pallas as pl
from jax.experimental.pallas import tpu as pltpu
from jax.sharding import PartitionSpec as P

SMOOTH_X = 32
SMOOTH_YZ = 4
COEFS = (8.0 / 5.0, -1.0 / 5.0, 8.0 / 315.0, -1.0 / 560.0)
CENTER = -205.0 / 72.0
REACH = 4
HIGHEST = lax.Precision.HIGHEST
MESH = pl.DeviceIdType.MESH

SCALE = 5040.0
WHOLE = tuple(float(round(SCALE * weight)) for weight in COEFS)
MIDDLE = 3.0 * float(round(SCALE * CENTER))

VMEM = pl.BlockSpec(memory_space=pltpu.VMEM)
SMEM = pl.BlockSpec(memory_space=pltpu.SMEM)
HBM = pl.BlockSpec(memory_space=pltpu.HBM)


def smoothing_table(length, strength):
    counter = np.arange(1, length + 1, dtype=np.float64)
    sines = np.sin(np.pi * np.outer(counter, counter) / (length + 1))
    half_sine = np.sin(np.pi * counter / (2 * (length + 1)))
    resp = 1.0 / (1.0 + strength * 4.0 * half_sine**2)
    table = 2.0 / (length + 1) * (sines * resp[None, :]) @ sines
    return table, 1.0 / math.sqrt(np.mean(resp * resp))


def stencil_tables(width_y, width_z):
    def bands(length):
        return sum(
            weight * (np.eye(length, k=offset + 1) + np.eye(length, k=-offset - 1))
            for offset, weight in enumerate(WHOLE)
        )

    band_y = bands(width_y)
    band_z = np.kron(np.eye(2), bands(width_z))
    return (
        jnp.asarray(np.concatenate([band_y, band_y], axis=1), jnp.bfloat16),
        jnp.asarray(np.concatenate([band_z, band_z], axis=0), jnp.bfloat16),
    )


def split(cell, width):
    if width & (width - 1) == 0:
        return cell >> (width.bit_length() - 1), cell & (width - 1)
    return lax.div(cell, width), lax.rem(cell, width)


def inject_kernel(
    packed, rec_data, src_sign, wavelet, late, now,
    late_out, now_out, first_out, second_out,
    late_buf, now_buf, first_buf, second_buf,
    cells, rec_values, src_signs, src_values, picks, sems,
):
    size, width = math.prod(late.shape), late.shape[1]
    rows = size // width
    bits = cell_bits(size, width)
    whole = pl.ds(0, rows)
    moves = [
        (packed, cells), (rec_data, rec_values), (src_sign, src_signs), (wavelet, src_values),
        (late, late_buf.at[whole]), (now, now_buf.at[whole]),
        (first_buf.at[whole], first_out), (second_buf.at[whole], second_out),
        (late_buf.at[whole], late_out), (now_buf.at[whole], now_out),
    ]
    copies = [
        pltpu.make_async_copy(source, target, sems.at[index])
        for index, (source, target) in enumerate(moves)
    ]
    for copy in copies[:6]:
        copy.start()
    step = math.gcd(rows, 256)

    def clear(index, carry):
        place = pl.ds(pl.multiple_of(index * step, step), step)
        zero = jnp.zeros((step, width), jnp.float32)
        first_buf[place, :] = zero
        second_buf[place, :] = zero
        return carry

    lax.fori_loop(0, rows // step, clear, 0)
    lanes = lax.broadcasted_iota(jnp.int32, (1, width), 1)
    group = GROUP

    def choose(start, total):
        together = math.gcd(total, 32)

        def some(index, count):
            values = [cells[start + index * together + extra] for extra in range(together)]
            grows = [1 + (value >> 31) for value in values]
            for value, grow in zip(values, grows):
                picks[count] = value
                count += grow
            return count

        count = lax.fori_loop(0, total // together, some, 0)
        for extra in range(2 * group - 1):
            picks[count + extra] = size
        return count

    def add(count, amounts, outs, sign):
        def fetch(index):
            values = [picks[index * group + extra] for extra in range(group)]
            amount = tuple(amounts(value >> bits) for value in values)
            local = [value & ((1 << bits) - 1) for value in values]
            return tuple(split(cell, width) for cell in local), amount

        def some(index, carry):
            spots, amount = carry
            places, lane = zip(*spots)
            olds = [[out[pl.ds(place, 1), :] for place in places] for out in outs]
            masks = [lanes == column for column in lane]
            added = [
                [jnp.where(mask, pair[side], 0.0) for mask, pair in zip(masks, amount)]
                for side in range(len(outs))
            ]
            totals = [list(parts) for parts in added]
            for later in range(group):
                for early in range(later):
                    same = places[early] == places[later]
                    for side in range(len(outs)):
                        totals[side][later] += jnp.where(same, added[side][early], 0.0)
            for side, out in enumerate(outs):
                for place, old, total in zip(places, olds[side], totals[side]):
                    out[pl.ds(place, 1), :] = old + total if sign > 0 else old - total
            return fetch(index + 1)

        lax.fori_loop(0, lax.div(count + (group - 1), group), some, fetch(0))

    def source_values(item):
        sign = (2 * src_signs[0, item] - 1).astype(jnp.float32)
        return sign * src_values[0, 0, item], sign * src_values[0, 1, item]

    receivers, sources = rec_data.shape[-1], src_sign.shape[-1]
    for copy in copies[:4]:
        copy.wait()
    add(choose(receivers, sources), source_values, (first_buf, second_buf), 1)
    copies[6].start()
    copies[7].start()
    count = choose(0, receivers)
    copies[4].wait()
    copies[5].wait()
    add(count, lambda item: (rec_values[0, 0, item], rec_values[0, 1, item]), (late_buf, now_buf), -1)
    copies[8].start()
    copies[9].start()
    for copy in copies[6:]:
        copy.wait()


GROUP = 4


def cell_bits(size, width):
    return (size + width - 1).bit_length()


def inject(rec_cell, rec_data, src_cell, src_sign, wavelet, late, now):
    size, width = math.prod(late.shape), late.shape[1]
    bits = cell_bits(size, width)
    receivers, sources = rec_cell.shape[0], src_cell.shape[1]
    most = max(receivers, sources)
    assert bits + (most - 1).bit_length() <= 31
    items = np.concatenate([np.arange(receivers), np.arange(sources)]).astype(np.int32) << bits
    local = jnp.concatenate([rec_cell, src_cell[0]]) - lax.axis_index("mp") * size
    packed = jnp.where((local >= 0) & (local < size), local | items, -1)
    shape = jax.ShapeDtypeStruct(late.shape, jnp.float32)
    padded = pltpu.VMEM((late.shape[0] + 8, width), jnp.float32)
    small = (packed, rec_data, src_sign, wavelet)
    return pl.pallas_call(
        inject_kernel,
        out_shape=(shape,) * 4,
        in_specs=[HBM] * 6,
        out_specs=(HBM,) * 4,
        scratch_shapes=[padded] * 4
        + [pltpu.SMEM(array.shape, array.dtype) for array in small]
        + [pltpu.SMEM((most + 2 * GROUP,), jnp.int32), pltpu.SemaphoreType.DMA((10,))],
        compiler_params=pltpu.CompilerParams(vmem_limit_bytes=VMEM_GRANT),
        name="inject",
    )(*small, late, now)


def slab_tables(table, count, order):
    rows = table.shape[0] // count
    mixes, sums = [], []
    for me in range(count):
        own = slice(me * rows, (me + 1) * rows)
        sums.append(np.stack([table[me * rows, own][order], table[(me + 1) * rows - 1, own][order]]))
        columns = [table[own, own][:, order]]
        for shift in range(1, count):
            source = (me - shift) % count
            seen = (source + 1) * rows - 1 if source < me else source * rows
            columns.append((table[own, seen] / table[seen, seen])[:, None])
        mixes.append(np.concatenate(columns, axis=1))
    return (
        jnp.asarray(np.stack(mixes).reshape(-1), jnp.float32),
        jnp.asarray(np.stack(sums).reshape(-1), jnp.float32),
    )


def make_kernel(slabs, groups, rows, width_y, width_z):
    blocks = rows // REACH
    chips = groups // 2
    lines = width_y // groups
    lanes = max(lines, min(128, REACH * lines))
    group = lanes // lines
    ratio = slabs // groups
    deep = width_z // slabs
    parts = ((rows - 2 * REACH) // group, 2 * REACH // group)
    starts = (0, parts[0])
    total_places = sum(parts)
    total_rows = ratio * rows
    ready_planes = slabs * total_places * deep * lanes // (width_y * width_z)

    def kernel(
        f_hbm, a_hbm, old_hbm, courant_hbm, late_hbm, now_hbm, first_hbm, second_hbm,
        table_y, table_z, smooth_y, smooth_z, sums,
        raw_out, lined, planes_in,
        raw, fbuf, abuf, obuf, cbuf, nbuf, mbuf, lbuf, sbuf, halo_one, halo_two,
        pair_in, chip_in, arrived, spread, planes,
        load_sem, one_send, one_recv, two_send, two_recv, pair_send, pair_recv,
        chip_send, chip_recv, turn_send, turn_recv, plane_send, plane_recv,
    ):
        m, s = lax.axis_index("mp"), lax.axis_index("shot")
        core = lax.rem(s, 2)
        chip = lax.div(s, 2)
        exists = (m > 0, m < slabs - 1)
        beside = (m - 1, m + 1)
        partner = s + 1 - 2 * core

        inner = list(range(2, blocks - 2))
        near = [block for block in (1, blocks - 2) if 0 < block < blocks - 1]
        near = sorted(set(near) - set(inner))
        edges = [0, blocks - 1]

        barrier = pltpu.get_barrier_semaphore()
        peers = slabs * groups
        me = m * groups + s

        def greet(index, carry):
            other = lax.rem(me + index, peers)
            pl.semaphore_signal(
                barrier, inc=1,
                device_id={"mp": lax.div(other, groups), "shot": lax.rem(other, groups)},
                device_id_type=MESH,
            )
            return carry

        lax.fori_loop(1, peers, greet, 0)

        term = abuf.reshape(rows + 2 * REACH, chips, 2, lines, width_z)
        pair = fbuf.at[: rows // 2].reshape(rows, chips, lines, width_z)
        ready = fbuf.at[rows // 2 : rows // 2 + ready_planes].reshape(slabs, total_places, deep, lanes)
        buffers = (
            (f_hbm, fbuf, REACH), (a_hbm, abuf, REACH), (old_hbm, obuf, 0), (courant_hbm, cbuf, 0),
            (late_hbm, lbuf, 0), (first_hbm, sbuf, 0), (now_hbm, lbuf, 0), (second_hbm, sbuf, 0),
        )

        def load(which, block):
            source, target, pad = buffers[which]
            return pltpu.make_async_copy(
                source.at[pl.ds(block * REACH, REACH)],
                target.at[pl.ds(block * REACH + pad, REACH)],
                load_sem.at[which, block],
            )

        for block in range(blocks):
            for which in range(6):
                load(which, block).start()
        for buf in (fbuf, abuf, nbuf, mbuf):
            zero = jnp.zeros((REACH,) + buf.shape[1:], jnp.float32)
            buf[:REACH] = zero
            buf[REACH + rows :] = zero

        pl.semaphore_wait(barrier, peers - 1)

        def one_copy(side, field, reach):
            row = reach if side == 0 else rows - 1 - reach
            return pltpu.make_async_remote_copy(
                src_ref=(f_hbm, a_hbm)[field].at[row],
                dst_ref=halo_one.at[1 - side, field, reach],
                send_sem=one_send.at[side, field, reach],
                recv_sem=one_recv.at[1 - side, field, reach],
                device_id={"mp": beside[side]},
                device_id_type=MESH,
            )

        def two_copy(side, field, reach):
            row = reach if side == 0 else rows - 1 - reach
            return pltpu.make_async_remote_copy(
                src_ref=(nbuf, mbuf)[field].at[REACH + row],
                dst_ref=halo_two.at[1 - side, field, reach],
                send_sem=two_send.at[side, field, reach],
                recv_sem=two_recv.at[1 - side, field, reach],
                device_id={"mp": beside[side]},
                device_id_type=MESH,
            )

        def landed(buffer, sem, side, field, reach):
            ref = buffer.at[side, field, reach]
            return pltpu.make_async_copy(ref, ref, sem.at[side, field, reach])

        for side in range(2):

            @pl.when(exists[side])
            def _():
                for reach in range(REACH):
                    for field in range(2):
                        one_copy(side, field, reach).start()

        spread[...] = jnp.zeros(spread.shape, jnp.float32)
        for source in range(groups):
            for part in range(group):
                top = source * lanes + part * lines
                spread[top : top + lines, part * width_y : (part + 1) * width_y] = smooth_y[
                    source * lines : (source + 1) * lines, :
                ]

        def laplace(place, fields):
            centers = [field[place] for field in fields]
            both = jnp.concatenate(centers, axis=1)
            high = both.astype(jnp.bfloat16)
            low = (both - high.astype(jnp.float32)).astype(jnp.bfloat16)
            total = jnp.dot(
                table_y[...], jnp.concatenate([high, low], axis=0), preferred_element_type=jnp.float32
            ) + jnp.dot(
                jnp.concatenate([high, low], axis=1), table_z[...], preferred_element_type=jnp.float32
            )
            laps = []
            for side, field in enumerate(fields):
                lap = total[:, side * width_z : (side + 1) * width_z] + MIDDLE * centers[side]
                for offset, weight in enumerate(WHOLE):
                    lap += weight * (field[place + offset + 1] + field[place - offset - 1])
                laps.append(lap)
            return centers, laps

        def first_block(block, carry):
            @pl.when(block + 1 < blocks)
            def _():
                for which in range(6):
                    load(which, block + 1).wait()

            for extra in range(REACH):
                row = block * REACH + extra
                (f_row, a_row), (lap_f, lap_a) = laplace(row + REACH, (fbuf, abuf))
                here = cbuf[row] * (1.0 / SCALE)
                accel = here * lap_f + sbuf[row]
                nbuf[row + REACH] = (2.0 * f_row - obuf[row]) + accel
                obuf[row] = accel
                mbuf[row + REACH] = (2.0 * a_row - lbuf[row]) + here * lap_a
            return carry

        for which in range(6):
            load(which, 0).wait()
        lax.fori_loop(0, blocks, first_block, 0)
        for block in inner + near + edges:
            for which in (6, 7):
                load(which, block).start()

        def first_edge(reach):
            for side in range(2):

                @pl.when(exists[side])
                def _():
                    for field in range(2):
                        landed(halo_one, one_recv, side, field, reach).wait()
                    for near in range(REACH - reach):
                        row = near if side == 0 else rows - 1 - near
                        here = COEFS[reach + near] * cbuf[row]
                        add_f = here * halo_one[side, 0, reach]
                        obuf[row] += add_f
                        nbuf[row + REACH] += add_f
                        mbuf[row + REACH] += here * halo_one[side, 1, reach]
                    for field in range(2):
                        two_copy(side, field, REACH - 1 - reach).start()

        def second_block(block):
            for which in (6, 7):
                load(which, block).wait()
            for extra in range(REACH):
                row = block * REACH + extra
                (_, a_row), (lap_f, lap_a) = laplace(row + REACH, (nbuf, mbuf))
                here = cbuf[row] * (1.0 / SCALE)
                accel_second = here * lap_f + sbuf[row]
                a_first = (2.0 * a_row - lbuf[row]) + here * lap_a
                value = a_first * obuf[row] + a_row * accel_second
                term[row] = value.reshape(chips, 2, lines, width_z)

        def pair_copy(block):
            return pltpu.make_async_remote_copy(
                src_ref=term.at[pl.ds(block * REACH, REACH), :, 1 - core],
                dst_ref=pair_in.at[pl.ds(block * REACH, REACH)],
                send_sem=pair_send.at[block],
                recv_sem=pair_recv.at[block],
                device_id={"shot": partner},
                device_id_type=MESH,
            )

        def chip_copy(shift, block):
            other = lax.rem(chip + shift, chips)
            return pltpu.make_async_remote_copy(
                src_ref=pair.at[pl.ds(block * REACH, REACH), other],
                dst_ref=chip_in.at[shift - 1, pl.ds(block * REACH, REACH)],
                send_sem=chip_send.at[shift - 1, block],
                recv_sem=chip_recv.at[shift - 1, block],
                device_id={"shot": other * 2 + core},
                device_id_type=MESH,
            )

        def add_pair(block):
            pair_copy(block).wait_recv()
            here = pl.ds(block * REACH, REACH)
            pair[here] = term[here, :, core] + pair_in[here]
            for shift in range(1, chips):
                chip_copy(shift, block).start()

        def add_chips(block):
            here = pl.ds(block * REACH, REACH)
            value = pair[here, chip]
            for shift in range(1, chips):
                chip_copy(shift, block).wait_recv()
                value += chip_in[shift - 1, here]
            raw[here] = value / float(groups)

        def turn_rows(start, count, place):
            turned = lax.dot_general(
                smooth_z[...],
                raw[start : start + count].reshape(count * lines, width_z),
                (((1,), (1,)), ((), ())),
                precision=HIGHEST,
                preferred_element_type=jnp.float32,
            )
            for index in range(count // group):
                for target in range(slabs):
                    ready[target, place + index] = turned[
                        target * deep : (target + 1) * deep, index * lanes : (index + 1) * lanes
                    ]

        goal = lax.div(m, ratio)
        slot = lax.rem(m, ratio) * groups + s

        def turn_copy(part, shift):
            target = lax.rem(m + shift, slabs)
            place = pl.ds(starts[part], parts[part])
            return pltpu.make_async_remote_copy(
                src_ref=ready.at[target, place],
                dst_ref=arrived.at[slot, place],
                send_sem=turn_send.at[part, target],
                recv_sem=turn_recv.at[part, slot],
                device_id={"mp": target, "shot": goal},
                device_id_type=MESH,
            )

        def turn_start(part):
            for shift in range(1, slabs):
                turn_copy(part, shift).start()

            @pl.when(s != goal)
            def _():
                turn_copy(part, 0).start()

            @pl.when(s == goal)
            def _():
                place = pl.ds(starts[part], parts[part])
                pltpu.make_async_copy(
                    ready.at[m, place], arrived.at[slot, place], turn_recv.at[part, slot]
                ).start()

        def turn_wait(part):
            place = pl.ds(starts[part], parts[part])
            for index in range(ratio * groups):
                ref = arrived.at[index, place]
                pltpu.make_async_copy(ref, ref, turn_recv.at[part, index]).wait()

        first_edge(0)
        first_edge(1)
        for block in inner:
            second_block(block)
            pair_copy(block).start()
        first_edge(2)
        for block in inner:
            add_pair(block)
        first_edge(3)
        for block in near:
            second_block(block)
            pair_copy(block).start()
        for block in edges:
            second_block(block)
        for block in near:
            add_pair(block)
        for block in inner + near:
            add_chips(block)
        turn_rows(REACH, rows - 2 * REACH, 0)

        for reach in reversed(range(REACH)):
            for side in range(2):

                @pl.when(exists[side])
                def _():
                    for field in range(2):
                        landed(halo_two, two_recv, side, field, reach).wait()
                    for close in range(REACH - reach):
                        row = close if side == 0 else rows - 1 - close
                        here = COEFS[reach + close] * cbuf[row]
                        extra = halo_two[side, 1, reach] * obuf[row] + mbuf[row + REACH] * halo_two[side, 0, reach]
                        term[row] += (here * extra).reshape(chips, 2, lines, width_z)

        for block in edges:
            pair_copy(block).start()

        @pl.when(chip == lax.div(goal, 2))
        def _():
            turn_start(0)

        for block in edges:
            add_pair(block)

        @pl.when(chip != lax.div(goal, 2))
        def _():
            turn_start(0)

        for block in edges:
            add_chips(block)
        turn_rows(0, REACH, parts[0])
        turn_rows(rows - REACH, REACH, parts[0] + REACH // group)
        turn_start(1)
        raw_copy = pltpu.make_async_copy(raw, raw_out, load_sem.at[0, 0])
        raw_copy.start()

        turn_wait(0)
        turn_wait(1)
        for index in range(ratio):
            joined = jnp.concatenate(
                [
                    arrived[index * groups + source].reshape(total_places * deep, lanes)
                    for source in range(groups)
                ],
                axis=1,
            )
            done = jnp.dot(joined, spread[...], precision=HIGHEST, preferred_element_type=jnp.float32)
            for place in range(total_places):
                for part in range(group):
                    lined[(index * total_places + place) * group + part] = done[
                        place * deep : (place + 1) * deep, part * width_y : (part + 1) * width_y
                    ]
        base = s * (2 * total_rows)
        for side in range(2):
            sum_side = sums[base + side * total_rows] * lined[0]
            for row in range(1, total_rows):
                sum_side += sums[base + side * total_rows + row] * lined[row]
            planes[side] = sum_side

        def plane_copy(shift):
            upward = jnp.where(s + shift < groups, 1, 0)
            return pltpu.make_async_remote_copy(
                src_ref=planes.at[upward],
                dst_ref=planes_in.at[shift - 1],
                send_sem=plane_send.at[shift - 1],
                recv_sem=plane_recv.at[shift - 1],
                device_id={"shot": lax.rem(s + shift, groups)},
                device_id_type=MESH,
            )

        for shift in range(1, groups):
            plane_copy(shift).start()
        for shift in range(1, groups):
            plane_copy(shift).wait_recv()
        for side in range(2):

            @pl.when(exists[side])
            def _():
                for reach in range(REACH):
                    for field in range(2):
                        one_copy(side, field, reach).wait_send()
                        two_copy(side, field, reach).wait_send()

        for block in range(blocks):
            pair_copy(block).wait_send()
            for shift in range(1, chips):
                chip_copy(shift, block).wait_send()
        for part in range(2):
            for shift in range(1, slabs):
                turn_copy(part, shift).wait_send()

            @pl.when(s != goal)
            def _():
                turn_copy(part, 0).wait_send()

        for shift in range(1, groups):
            plane_copy(shift).wait_send()
        raw_copy.wait()

    padded = pltpu.VMEM((rows + 2 * REACH, width_y, width_z), jnp.float32)
    slab = pltpu.VMEM((rows, width_y, width_z), jnp.float32)
    halo = pltpu.VMEM((2, 2, REACH, width_y, width_z), jnp.float32)
    dma = pltpu.SemaphoreType.DMA
    scratch = [
        pltpu.VMEM((rows, lines, width_z), jnp.float32),
        padded, padded, slab, slab, padded, padded, slab, slab,
        halo, halo,
        pltpu.VMEM((rows, chips, lines, width_z), jnp.float32),
        pltpu.VMEM((max(1, chips - 1), rows, lines, width_z), jnp.float32),
        pltpu.VMEM((ratio * groups, total_places, deep, lanes), jnp.float32),
        pltpu.VMEM((groups * lanes, group * width_y), jnp.float32),
        pltpu.VMEM((2, deep, width_y), jnp.float32),
        dma((8, blocks)),
        dma((2, 2, REACH)), dma((2, 2, REACH)), dma((2, 2, REACH)), dma((2, 2, REACH)),
        dma((blocks,)), dma((blocks,)),
        dma((max(1, chips - 1), blocks)), dma((max(1, chips - 1), blocks)),
        dma((2, slabs)), dma((2, ratio * groups)),
        dma((groups - 1,)), dma((groups - 1,)),
    ]
    outs = (
        jax.ShapeDtypeStruct((rows, lines, width_z), jnp.float32),
        jax.ShapeDtypeStruct((total_rows, deep, width_y), jnp.float32),
        jax.ShapeDtypeStruct((groups - 1, deep, width_y), jnp.float32),
    )
    inner_rows = list(range(REACH, rows - REACH)) + list(range(REACH)) + list(range(rows - REACH, rows))
    order = np.concatenate([index * rows + np.array(inner_rows) for index in range(ratio)])
    return kernel, scratch, outs, order


def mix_kernel(
    raw_hbm, lined, planes, mix, raw_out, smooth, raw, buffer, sems
):
    total_rows, others = lined.shape[0], planes.shape[0]
    wide = total_rows + others
    step = math.gcd(total_rows, 4)
    base = lax.axis_index("shot") * total_rows
    fetch = pltpu.make_async_copy(raw_hbm, raw, sems.at[0])
    fetch.start()
    store = pltpu.make_async_copy(raw, raw_out, sems.at[1])

    def write(index):
        here = pl.ds(index * step, step)
        return pltpu.make_async_copy(buffer.at[here], smooth.at[here], sems.at[index + 2])

    def some(index, carry):
        totals = [None] * step
        for source in range(wide):
            value = lined[source] if source < total_rows else planes[source - total_rows]
            for extra in range(step):
                piece = mix[(base + index * step + extra) * wide + source] * value
                totals[extra] = piece if source == 0 else totals[extra] + piece
        for extra in range(step):
            buffer[index * step + extra] = totals[extra]
        write(index).start()
        return carry

    fetch.wait()
    store.start()
    lax.fori_loop(0, total_rows // step, some, 0)
    for index in range(total_rows // step):
        write(index).wait()
    store.wait()


def mix_planes(raw, lined, planes, mix):
    steps = lined.shape[0] // math.gcd(lined.shape[0], 4)
    return pl.pallas_call(
        mix_kernel,
        out_shape=(
            jax.ShapeDtypeStruct(raw.shape, jnp.float32),
            jax.ShapeDtypeStruct(lined.shape, jnp.float32),
        ),
        in_specs=[HBM, VMEM, VMEM, SMEM],
        out_specs=(HBM, HBM),
        scratch_shapes=[
            pltpu.VMEM(raw.shape, jnp.float32), pltpu.VMEM(lined.shape, jnp.float32),
            pltpu.SemaphoreType.DMA((steps + 2,)),
        ],
        compiler_params=pltpu.CompilerParams(vmem_limit_bytes=MIX_GRANT),
        name="mix",
    )(raw, lined, planes, mix)


def per_device(
    courant, forward_old, forward_now, adjoint_late, adjoint_now,
    src_cell, src_sign, wavelet, rec_cell, rec_data,
):
    rows, width_y, width_z = courant.shape
    slabs, groups = lax.axis_size("mp"), lax.axis_size("shot")
    flat = (rows * width_y, width_z)
    injected = inject(
        rec_cell, rec_data, src_cell, src_sign, wavelet,
        adjoint_late.reshape(flat), adjoint_now.reshape(flat),
    )
    kernel, scratch, outs, order = make_kernel(slabs, groups, rows, width_y, width_z)
    table_x, spread_x = smoothing_table(rows * slabs, SMOOTH_X**2)
    smooth_y, spread_y = smoothing_table(width_y, SMOOTH_YZ**2)
    smooth_z, spread_z = smoothing_table(width_z, SMOOTH_YZ**2)
    smooth_y = smooth_y * (spread_x * spread_y * spread_z)
    mix, sums = slab_tables(table_x, groups, order)
    raw, lined, planes = pl.pallas_call(
        kernel,
        out_shape=outs,
        in_specs=[HBM] * 8 + [VMEM] * 4 + [SMEM],
        out_specs=(HBM, VMEM, VMEM),
        scratch_shapes=scratch,
        compiler_params=pltpu.CompilerParams(
            collective_id=0, has_side_effects=True, vmem_limit_bytes=GRADIENT_GRANT
        ),
        name="gradient",
    )(
        forward_now[0], adjoint_now[0], forward_old[0], courant,
        *(array.reshape(rows, width_y, width_z) for array in injected),
        *stencil_tables(width_y, width_z),
        jnp.asarray(smooth_y, jnp.float32), jnp.asarray(smooth_z, jnp.float32),
        sums,
    )
    raw, smooth = mix_planes(raw, lined, planes, mix)
    return raw, jnp.swapaxes(smooth, 1, 2)


VMEM_GRANT = 60 * 2**20
GRADIENT_GRANT = 55 * 2**20
MIX_GRANT = 56 * 2**20


def solution(mesh):
    step = jax.shard_map(
        per_device,
        mesh=mesh,
        in_specs=(
            P(("parts", "mp"), None, None),
            P(("parts", "shot"), "mp", None, None),
            P(("parts", "shot"), "mp", None, None),
            P(("parts", "shot"), "mp", None, None),
            P(("parts", "shot"), "mp", None, None),
            P(("parts", "shot"), None),
            P(("parts", "shot"), None),
            P(("parts", "shot"), None, None),
            P("parts"),
            P(("parts", "shot"), None, None),
        ),
        out_specs=(P(("parts", "mp"), "shot", None), P(("parts", "shot"), None, "mp")),
        check_vma=False,
    )
    return step
```

```python
import math

import jax
import jax.numpy as jnp
import numpy as np
from jax import lax
from jax.experimental import pallas as pl
from jax.experimental.pallas import tpu as pltpu
from jax.sharding import PartitionSpec as P

SMOOTH_X = 32
SMOOTH_YZ = 4
COEFS = (8.0 / 5.0, -1.0 / 5.0, 8.0 / 315.0, -1.0 / 560.0)
CENTER = -205.0 / 72.0
REACH = 4
HIGHEST = lax.Precision.HIGHEST
MESH = pl.DeviceIdType.MESH

SCALE = 5040.0
WHOLE = tuple(float(round(SCALE * weight)) for weight in COEFS)
MIDDLE = 3.0 * float(round(SCALE * CENTER))

VMEM = pl.BlockSpec(memory_space=pltpu.VMEM)
SMEM = pl.BlockSpec(memory_space=pltpu.SMEM)
HBM = pl.BlockSpec(memory_space=pltpu.HBM)


def smoothing_table(length, strength):
    counter = np.arange(1, length + 1, dtype=np.float64)
    sines = np.sin(np.pi * np.outer(counter, counter) / (length + 1))
    half_sine = np.sin(np.pi * counter / (2 * (length + 1)))
    resp = 1.0 / (1.0 + strength * 4.0 * half_sine**2)
    table = 2.0 / (length + 1) * (sines * resp[None, :]) @ sines
    return table, 1.0 / math.sqrt(np.mean(resp * resp))


def stencil_tables(width_y, width_z):
    def bands(length):
        return sum(
            weight * (np.eye(length, k=offset + 1) + np.eye(length, k=-offset - 1))
            for offset, weight in enumerate(WHOLE)
        )

    band_y = bands(width_y)
    band_z = np.kron(np.eye(2), bands(width_z))
    return (
        jnp.asarray(np.concatenate([band_y, band_y], axis=1), jnp.bfloat16),
        jnp.asarray(np.concatenate([band_z, band_z], axis=0), jnp.bfloat16),
    )


def split(cell, width):
    if width & (width - 1) == 0:
        return cell >> (width.bit_length() - 1), cell & (width - 1)
    return lax.div(cell, width), lax.rem(cell, width)


def inject_kernel(
    packed, rec_data, src_sign, wavelet, late, now,
    late_out, now_out, first_out, second_out,
    late_buf, now_buf, first_buf, second_buf,
    cells, rec_values, src_signs, src_values, picks, sems,
):
    size, width = math.prod(late.shape), late.shape[1]
    rows = size // width
    bits = cell_bits(size, width)
    whole = pl.ds(0, rows)
    moves = [
        (packed, cells), (rec_data, rec_values), (src_sign, src_signs), (wavelet, src_values),
        (late, late_buf.at[whole]), (now, now_buf.at[whole]),
        (first_buf.at[whole], first_out), (second_buf.at[whole], second_out),
        (late_buf.at[whole], late_out), (now_buf.at[whole], now_out),
    ]
    copies = [
        pltpu.make_async_copy(source, target, sems.at[index])
        for index, (source, target) in enumerate(moves)
    ]
    for copy in copies[:6]:
        copy.start()
    step = math.gcd(rows, 256)

    def clear(index, carry):
        place = pl.ds(pl.multiple_of(index * step, step), step)
        zero = jnp.zeros((step, width), jnp.float32)
        first_buf[place, :] = zero
        second_buf[place, :] = zero
        return carry

    lax.fori_loop(0, rows // step, clear, 0)
    lanes = lax.broadcasted_iota(jnp.int32, (1, width), 1)
    group = GROUP

    def choose(start, total):
        together = math.gcd(total, 8)

        def some(index, count):
            values = [cells[start + index * together + extra] for extra in range(together)]
            grows = [1 + (value >> 31) for value in values]
            for value, grow in zip(values, grows):
                picks[count] = value
                count += grow
            return count

        count = lax.fori_loop(0, total // together, some, 0)
        for extra in range(2 * group - 1):
            picks[count + extra] = size
        return count

    def add(count, amounts, outs, sign):
        def fetch(index):
            values = [picks[index * group + extra] for extra in range(group)]
            amount = tuple(amounts(value >> bits) for value in values)
            local = [value & ((1 << bits) - 1) for value in values]
            return tuple(split(cell, width) for cell in local), amount

        def some(index, carry):
            spots, amount = carry
            places, lane = zip(*spots)
            olds = [[out[pl.ds(place, 1), :] for place in places] for out in outs]
            masks = [lanes == column for column in lane]
            added = [
                [jnp.where(mask, pair[side], 0.0) for mask, pair in zip(masks, amount)]
                for side in range(len(outs))
            ]
            totals = [list(parts) for parts in added]
            for later in range(group):
                for early in range(later):
                    same = places[early] == places[later]
                    for side in range(len(outs)):
                        totals[side][later] += jnp.where(same, added[side][early], 0.0)
            for side, out in enumerate(outs):
                for place, old, total in zip(places, olds[side], totals[side]):
                    out[pl.ds(place, 1), :] = old + total if sign > 0 else old - total
            return fetch(index + 1)

        lax.fori_loop(0, lax.div(count + (group - 1), group), some, fetch(0))

    def source_values(item):
        sign = (2 * src_signs[0, item] - 1).astype(jnp.float32)
        return sign * src_values[0, 0, item], sign * src_values[0, 1, item]

    receivers, sources = rec_data.shape[-1], src_sign.shape[-1]
    for copy in copies[:4]:
        copy.wait()
    add(choose(receivers, sources), source_values, (first_buf, second_buf), 1)
    copies[6].start()
    copies[7].start()
    count = choose(0, receivers)
    copies[4].wait()
    copies[5].wait()
    add(count, lambda item: (rec_values[0, 0, item], rec_values[0, 1, item]), (late_buf, now_buf), -1)
    copies[8].start()
    copies[9].start()
    for copy in copies[6:]:
        copy.wait()


GROUP = 4


def cell_bits(size, width):
    return (size + width - 1).bit_length()


def inject(rec_cell, rec_data, src_cell, src_sign, wavelet, late, now):
    size, width = math.prod(late.shape), late.shape[1]
    bits = cell_bits(size, width)
    receivers, sources = rec_cell.shape[0], src_cell.shape[1]
    most = max(receivers, sources)
    assert bits + (most - 1).bit_length() <= 31
    items = np.concatenate([np.arange(receivers), np.arange(sources)]).astype(np.int32) << bits
    local = jnp.concatenate([rec_cell, src_cell[0]]) - lax.axis_index("mp") * size
    packed = jnp.where((local >= 0) & (local < size), local | items, -1)
    shape = jax.ShapeDtypeStruct(late.shape, jnp.float32)
    padded = pltpu.VMEM((late.shape[0] + 8, width), jnp.float32)
    small = (packed, rec_data, src_sign, wavelet)
    return pl.pallas_call(
        inject_kernel,
        out_shape=(shape,) * 4,
        in_specs=[HBM] * 6,
        out_specs=(HBM,) * 4,
        scratch_shapes=[padded] * 4
        + [pltpu.SMEM(array.shape, array.dtype) for array in small]
        + [pltpu.SMEM((most + 2 * GROUP,), jnp.int32), pltpu.SemaphoreType.DMA((10,))],
        compiler_params=pltpu.CompilerParams(vmem_limit_bytes=VMEM_GRANT),
        name="inject",
    )(*small, late, now)


def slab_tables(table, count, order):
    rows = table.shape[0] // count
    mixes, sums = [], []
    for me in range(count):
        own = slice(me * rows, (me + 1) * rows)
        sums.append(np.stack([table[me * rows, own][order], table[(me + 1) * rows - 1, own][order]]))
        columns = [table[own, own][:, order]]
        for shift in range(1, count):
            source = (me - shift) % count
            seen = (source + 1) * rows - 1 if source < me else source * rows
            columns.append((table[own, seen] / table[seen, seen])[:, None])
        mixes.append(np.concatenate(columns, axis=1))
    return (
        jnp.asarray(np.stack(mixes).reshape(-1), jnp.float32),
        jnp.asarray(np.stack(sums).reshape(-1), jnp.float32),
    )


def make_kernel(slabs, groups, rows, width_y, width_z):
    blocks = rows // REACH
    chips = groups // 2
    lines = width_y // groups
    lanes = max(lines, min(128, REACH * lines))
    group = lanes // lines
    ratio = slabs // groups
    deep = width_z // slabs
    parts = ((rows - 2 * REACH) // group, 2 * REACH // group)
    starts = (0, parts[0])
    total_places = sum(parts)
    total_rows = ratio * rows
    ready_planes = slabs * total_places * deep * lanes // (width_y * width_z)

    def kernel(
        f_hbm, a_hbm, old_hbm, courant_hbm, late_hbm, now_hbm, first_hbm, second_hbm,
        table_y, table_z, smooth_y, smooth_z, sums,
        raw_out, lined, planes_in,
        raw, fbuf, abuf, obuf, cbuf, nbuf, mbuf, lbuf, sbuf, halo_one, halo_two,
        pair_in, chip_in, arrived, spread, planes,
        load_sem, one_send, one_recv, two_send, two_recv, pair_send, pair_recv,
        chip_send, chip_recv, turn_send, turn_recv, plane_send, plane_recv,
    ):
        m, s = lax.axis_index("mp"), lax.axis_index("shot")
        core = lax.rem(s, 2)
        chip = lax.div(s, 2)
        exists = (m > 0, m < slabs - 1)
        beside = (m - 1, m + 1)
        partner = s + 1 - 2 * core

        inner = list(range(2, blocks - 2))
        near = [block for block in (1, blocks - 2) if 0 < block < blocks - 1]
        near = sorted(set(near) - set(inner))
        edges = [0, blocks - 1]

        barrier = pltpu.get_barrier_semaphore()
        peers = slabs * groups
        me = m * groups + s

        def greet(index, carry):
            other = lax.rem(me + index, peers)
            pl.semaphore_signal(
                barrier, inc=1,
                device_id={"mp": lax.div(other, groups), "shot": lax.rem(other, groups)},
                device_id_type=MESH,
            )
            return carry

        lax.fori_loop(1, peers, greet, 0)

        term = abuf.reshape(rows + 2 * REACH, chips, 2, lines, width_z)
        pair = fbuf.at[: rows // 2].reshape(rows, chips, lines, width_z)
        ready = fbuf.at[rows // 2 : rows // 2 + ready_planes].reshape(slabs, total_places, deep, lanes)
        buffers = (
            (f_hbm, fbuf, REACH), (a_hbm, abuf, REACH), (old_hbm, obuf, 0), (courant_hbm, cbuf, 0),
            (late_hbm, lbuf, 0), (first_hbm, sbuf, 0), (now_hbm, lbuf, 0), (second_hbm, sbuf, 0),
        )

        def load(which, block):
            source, target, pad = buffers[which]
            return pltpu.make_async_copy(
                source.at[pl.ds(block * REACH, REACH)],
                target.at[pl.ds(block * REACH + pad, REACH)],
                load_sem.at[which, block],
            )

        for block in range(blocks):
            for which in range(6):
                load(which, block).start()
        for buf in (fbuf, abuf, nbuf, mbuf):
            zero = jnp.zeros((REACH,) + buf.shape[1:], jnp.float32)
            buf[:REACH] = zero
            buf[REACH + rows :] = zero

        pl.semaphore_wait(barrier, peers - 1)

        def one_copy(side, field, reach):
            row = reach if side == 0 else rows - 1 - reach
            return pltpu.make_async_remote_copy(
                src_ref=(f_hbm, a_hbm)[field].at[row],
                dst_ref=halo_one.at[1 - side, field, reach],
                send_sem=one_send.at[side, field, reach],
                recv_sem=one_recv.at[1 - side, field, reach],
                device_id={"mp": beside[side]},
                device_id_type=MESH,
            )

        def two_copy(side, field, reach):
            row = reach if side == 0 else rows - 1 - reach
            return pltpu.make_async_remote_copy(
                src_ref=(nbuf, mbuf)[field].at[REACH + row],
                dst_ref=halo_two.at[1 - side, field, reach],
                send_sem=two_send.at[side, field, reach],
                recv_sem=two_recv.at[1 - side, field, reach],
                device_id={"mp": beside[side]},
                device_id_type=MESH,
            )

        def landed(buffer, sem, side, field, reach):
            ref = buffer.at[side, field, reach]
            return pltpu.make_async_copy(ref, ref, sem.at[side, field, reach])

        for side in range(2):

            @pl.when(exists[side])
            def _():
                for reach in range(REACH):
                    for field in range(2):
                        one_copy(side, field, reach).start()

        spread[...] = jnp.zeros(spread.shape, jnp.float32)
        for source in range(groups):
            for part in range(group):
                top = source * lanes + part * lines
                spread[top : top + lines, part * width_y : (part + 1) * width_y] = smooth_y[
                    source * lines : (source + 1) * lines, :
                ]

        def laplace(place, fields):
            centers = [field[place] for field in fields]
            both = jnp.concatenate(centers, axis=1)
            high = both.astype(jnp.bfloat16)
            low = (both - high.astype(jnp.float32)).astype(jnp.bfloat16)
            total = jnp.dot(
                table_y[...], jnp.concatenate([high, low], axis=0), preferred_element_type=jnp.float32
            ) + jnp.dot(
                jnp.concatenate([high, low], axis=1), table_z[...], preferred_element_type=jnp.float32
            )
            laps = []
            for side, field in enumerate(fields):
                lap = total[:, side * width_z : (side + 1) * width_z] + MIDDLE * centers[side]
                for offset, weight in enumerate(WHOLE):
                    lap += weight * (field[place + offset + 1] + field[place - offset - 1])
                laps.append(lap)
            return centers, laps

        def first_block(block, carry):
            @pl.when(block + 1 < blocks)
            def _():
                for which in range(6):
                    load(which, block + 1).wait()

            for extra in range(REACH):
                row = block * REACH + extra
                (f_row, a_row), (lap_f, lap_a) = laplace(row + REACH, (fbuf, abuf))
                here = cbuf[row] * (1.0 / SCALE)
                accel = here * lap_f + sbuf[row]
                nbuf[row + REACH] = (2.0 * f_row - obuf[row]) + accel
                obuf[row] = accel
                mbuf[row + REACH] = (2.0 * a_row - lbuf[row]) + here * lap_a
            return carry

        for which in range(6):
            load(which, 0).wait()
        lax.fori_loop(0, blocks, first_block, 0)
        for block in inner + near + edges:
            for which in (6, 7):
                load(which, block).start()

        def first_edge(reach):
            for side in range(2):

                @pl.when(exists[side])
                def _():
                    for field in range(2):
                        landed(halo_one, one_recv, side, field, reach).wait()
                    for near in range(REACH - reach):
                        row = near if side == 0 else rows - 1 - near
                        here = COEFS[reach + near] * cbuf[row]
                        add_f = here * halo_one[side, 0, reach]
                        obuf[row] += add_f
                        nbuf[row + REACH] += add_f
                        mbuf[row + REACH] += here * halo_one[side, 1, reach]
                    for field in range(2):
                        two_copy(side, field, REACH - 1 - reach).start()

        def second_block(block):
            for which in (6, 7):
                load(which, block).wait()
            for extra in range(REACH):
                row = block * REACH + extra
                (_, a_row), (lap_f, lap_a) = laplace(row + REACH, (nbuf, mbuf))
                here = cbuf[row] * (1.0 / SCALE)
                accel_second = here * lap_f + sbuf[row]
                a_first = (2.0 * a_row - lbuf[row]) + here * lap_a
                value = a_first * obuf[row] + a_row * accel_second
                term[row] = value.reshape(chips, 2, lines, width_z)

        def pair_copy(block):
            return pltpu.make_async_remote_copy(
                src_ref=term.at[pl.ds(block * REACH, REACH), :, 1 - core],
                dst_ref=pair_in.at[pl.ds(block * REACH, REACH)],
                send_sem=pair_send.at[block],
                recv_sem=pair_recv.at[block],
                device_id={"shot": partner},
                device_id_type=MESH,
            )

        def chip_copy(shift, block):
            other = lax.rem(chip + shift, chips)
            return pltpu.make_async_remote_copy(
                src_ref=pair.at[pl.ds(block * REACH, REACH), other],
                dst_ref=chip_in.at[shift - 1, pl.ds(block * REACH, REACH)],
                send_sem=chip_send.at[shift - 1, block],
                recv_sem=chip_recv.at[shift - 1, block],
                device_id={"shot": other * 2 + core},
                device_id_type=MESH,
            )

        def add_pair(block):
            pair_copy(block).wait_recv()
            here = pl.ds(block * REACH, REACH)
            pair[here] = term[here, :, core] + pair_in[here]
            for shift in range(1, chips):
                chip_copy(shift, block).start()

        def add_chips(block):
            here = pl.ds(block * REACH, REACH)
            value = pair[here, chip]
            for shift in range(1, chips):
                chip_copy(shift, block).wait_recv()
                value += chip_in[shift - 1, here]
            raw[here] = value / float(groups)

        def turn_rows(start, count, place):
            turned = lax.dot_general(
                smooth_z[...],
                raw[start : start + count].reshape(count * lines, width_z),
                (((1,), (1,)), ((), ())),
                precision=HIGHEST,
                preferred_element_type=jnp.float32,
            )
            for index in range(count // group):
                for target in range(slabs):
                    ready[target, place + index] = turned[
                        target * deep : (target + 1) * deep, index * lanes : (index + 1) * lanes
                    ]

        goal = lax.div(m, ratio)
        slot = lax.rem(m, ratio) * groups + s

        def turn_copy(part, shift):
            target = lax.rem(m + shift, slabs)
            place = pl.ds(starts[part], parts[part])
            return pltpu.make_async_remote_copy(
                src_ref=ready.at[target, place],
                dst_ref=arrived.at[slot, place],
                send_sem=turn_send.at[part, target],
                recv_sem=turn_recv.at[part, slot],
                device_id={"mp": target, "shot": goal},
                device_id_type=MESH,
            )

        def turn_start(part):
            for shift in range(1, slabs):
                turn_copy(part, shift).start()

            @pl.when(s != goal)
            def _():
                turn_copy(part, 0).start()

            @pl.when(s == goal)
            def _():
                place = pl.ds(starts[part], parts[part])
                pltpu.make_async_copy(
                    ready.at[m, place], arrived.at[slot, place], turn_recv.at[part, slot]
                ).start()

        def turn_wait(part):
            place = pl.ds(starts[part], parts[part])
            for index in range(ratio * groups):
                ref = arrived.at[index, place]
                pltpu.make_async_copy(ref, ref, turn_recv.at[part, index]).wait()

        first_edge(0)
        first_edge(1)
        for block in inner:
            second_block(block)
            pair_copy(block).start()
        first_edge(2)
        for block in inner:
            add_pair(block)
        first_edge(3)
        for block in near:
            second_block(block)
            pair_copy(block).start()
        for block in edges:
            second_block(block)
        for block in near:
            add_pair(block)
        for block in inner + near:
            add_chips(block)
        turn_rows(REACH, rows - 2 * REACH, 0)

        for reach in reversed(range(REACH)):
            for side in range(2):

                @pl.when(exists[side])
                def _():
                    for field in range(2):
                        landed(halo_two, two_recv, side, field, reach).wait()
                    for close in range(REACH - reach):
                        row = close if side == 0 else rows - 1 - close
                        here = COEFS[reach + close] * cbuf[row]
                        extra = halo_two[side, 1, reach] * obuf[row] + mbuf[row + REACH] * halo_two[side, 0, reach]
                        term[row] += (here * extra).reshape(chips, 2, lines, width_z)

        for block in edges:
            pair_copy(block).start()
        turn_start(0)
        for block in edges:
            add_pair(block)
        for block in edges:
            add_chips(block)
        turn_rows(0, REACH, parts[0])
        turn_rows(rows - REACH, REACH, parts[0] + REACH // group)
        turn_start(1)
        raw_copy = pltpu.make_async_copy(raw, raw_out, load_sem.at[0, 0])
        raw_copy.start()

        turn_wait(0)
        turn_wait(1)
        for index in range(ratio):
            joined = jnp.concatenate(
                [
                    arrived[index * groups + source].reshape(total_places * deep, lanes)
                    for source in range(groups)
                ],
                axis=1,
            )
            done = jnp.dot(joined, spread[...], precision=HIGHEST, preferred_element_type=jnp.float32)
            for place in range(total_places):
                for part in range(group):
                    lined[(index * total_places + place) * group + part] = done[
                        place * deep : (place + 1) * deep, part * width_y : (part + 1) * width_y
                    ]
        base = s * (2 * total_rows)
        for side in range(2):
            sum_side = sums[base + side * total_rows] * lined[0]
            for row in range(1, total_rows):
                sum_side += sums[base + side * total_rows + row] * lined[row]
            planes[side] = sum_side

        def plane_copy(shift):
            upward = jnp.where(s + shift < groups, 1, 0)
            return pltpu.make_async_remote_copy(
                src_ref=planes.at[upward],
                dst_ref=planes_in.at[shift - 1],
                send_sem=plane_send.at[shift - 1],
                recv_sem=plane_recv.at[shift - 1],
                device_id={"shot": lax.rem(s + shift, groups)},
                device_id_type=MESH,
            )

        for shift in range(1, groups):
            plane_copy(shift).start()
        for shift in range(1, groups):
            plane_copy(shift).wait_recv()
        for side in range(2):

            @pl.when(exists[side])
            def _():
                for reach in range(REACH):
                    for field in range(2):
                        one_copy(side, field, reach).wait_send()
                        two_copy(side, field, reach).wait_send()

        for block in range(blocks):
            pair_copy(block).wait_send()
            for shift in range(1, chips):
                chip_copy(shift, block).wait_send()
        for part in range(2):
            for shift in range(1, slabs):
                turn_copy(part, shift).wait_send()

            @pl.when(s != goal)
            def _():
                turn_copy(part, 0).wait_send()

        for shift in range(1, groups):
            plane_copy(shift).wait_send()
        raw_copy.wait()

    padded = pltpu.VMEM((rows + 2 * REACH, width_y, width_z), jnp.float32)
    slab = pltpu.VMEM((rows, width_y, width_z), jnp.float32)
    halo = pltpu.VMEM((2, 2, REACH, width_y, width_z), jnp.float32)
    dma = pltpu.SemaphoreType.DMA
    scratch = [
        pltpu.VMEM((rows, lines, width_z), jnp.float32),
        padded, padded, slab, slab, padded, padded, slab, slab,
        halo, halo,
        pltpu.VMEM((rows, chips, lines, width_z), jnp.float32),
        pltpu.VMEM((max(1, chips - 1), rows, lines, width_z), jnp.float32),
        pltpu.VMEM((ratio * groups, total_places, deep, lanes), jnp.float32),
        pltpu.VMEM((groups * lanes, group * width_y), jnp.float32),
        pltpu.VMEM((2, deep, width_y), jnp.float32),
        dma((8, blocks)),
        dma((2, 2, REACH)), dma((2, 2, REACH)), dma((2, 2, REACH)), dma((2, 2, REACH)),
        dma((blocks,)), dma((blocks,)),
        dma((max(1, chips - 1), blocks)), dma((max(1, chips - 1), blocks)),
        dma((2, slabs)), dma((2, ratio * groups)),
        dma((groups - 1,)), dma((groups - 1,)),
    ]
    outs = (
        jax.ShapeDtypeStruct((rows, lines, width_z), jnp.float32),
        jax.ShapeDtypeStruct((total_rows, deep, width_y), jnp.float32),
        jax.ShapeDtypeStruct((groups - 1, deep, width_y), jnp.float32),
    )
    inner_rows = list(range(REACH, rows - REACH)) + list(range(REACH)) + list(range(rows - REACH, rows))
    order = np.concatenate([index * rows + np.array(inner_rows) for index in range(ratio)])
    return kernel, scratch, outs, order


def mix_kernel(
    raw_hbm, lined, planes, mix, raw_out, smooth, raw, buffer, sems
):
    total_rows, others = lined.shape[0], planes.shape[0]
    wide = total_rows + others
    step = math.gcd(total_rows, 4)
    base = lax.axis_index("shot") * total_rows
    fetch = pltpu.make_async_copy(raw_hbm, raw, sems.at[0])
    fetch.start()
    store = pltpu.make_async_copy(raw, raw_out, sems.at[1])

    def write(index):
        here = pl.ds(index * step, step)
        return pltpu.make_async_copy(buffer.at[here], smooth.at[here], sems.at[index + 2])

    def some(index, carry):
        totals = [None] * step
        for source in range(wide):
            value = lined[source] if source < total_rows else planes[source - total_rows]
            for extra in range(step):
                piece = mix[(base + index * step + extra) * wide + source] * value
                totals[extra] = piece if source == 0 else totals[extra] + piece
        for extra in range(step):
            buffer[index * step + extra] = totals[extra]
        write(index).start()
        return carry

    half = total_rows // step // 2
    lax.fori_loop(0, half, some, 0)
    fetch.wait()
    store.start()
    lax.fori_loop(half, total_rows // step, some, 0)
    for index in range(total_rows // step):
        write(index).wait()
    store.wait()


def mix_planes(raw, lined, planes, mix):
    steps = lined.shape[0] // math.gcd(lined.shape[0], 4)
    return pl.pallas_call(
        mix_kernel,
        out_shape=(
            jax.ShapeDtypeStruct(raw.shape, jnp.float32),
            jax.ShapeDtypeStruct(lined.shape, jnp.float32),
        ),
        in_specs=[HBM, VMEM, VMEM, SMEM],
        out_specs=(HBM, HBM),
        scratch_shapes=[
            pltpu.VMEM(raw.shape, jnp.float32), pltpu.VMEM(lined.shape, jnp.float32),
            pltpu.SemaphoreType.DMA((steps + 2,)),
        ],
        compiler_params=pltpu.CompilerParams(vmem_limit_bytes=MIX_GRANT),
        name="mix",
    )(raw, lined, planes, mix)


def per_device(
    courant, forward_old, forward_now, adjoint_late, adjoint_now,
    src_cell, src_sign, wavelet, rec_cell, rec_data,
):
    rows, width_y, width_z = courant.shape
    slabs, groups = lax.axis_size("mp"), lax.axis_size("shot")
    flat = (rows * width_y, width_z)
    injected = inject(
        rec_cell, rec_data, src_cell, src_sign, wavelet,
        adjoint_late.reshape(flat), adjoint_now.reshape(flat),
    )
    kernel, scratch, outs, order = make_kernel(slabs, groups, rows, width_y, width_z)
    table_x, spread_x = smoothing_table(rows * slabs, SMOOTH_X**2)
    smooth_y, spread_y = smoothing_table(width_y, SMOOTH_YZ**2)
    smooth_z, spread_z = smoothing_table(width_z, SMOOTH_YZ**2)
    smooth_y = smooth_y * (spread_x * spread_y * spread_z)
    mix, sums = slab_tables(table_x, groups, order)
    raw, lined, planes = pl.pallas_call(
        kernel,
        out_shape=outs,
        in_specs=[HBM] * 8 + [VMEM] * 4 + [SMEM],
        out_specs=(HBM, VMEM, VMEM),
        scratch_shapes=scratch,
        compiler_params=pltpu.CompilerParams(
            collective_id=0, has_side_effects=True, vmem_limit_bytes=GRADIENT_GRANT
        ),
        name="gradient",
    )(
        forward_now[0], adjoint_now[0], forward_old[0], courant,
        *(array.reshape(rows, width_y, width_z) for array in injected),
        *stencil_tables(width_y, width_z),
        jnp.asarray(smooth_y, jnp.float32), jnp.asarray(smooth_z, jnp.float32),
        sums,
    )
    raw, smooth = mix_planes(raw, lined, planes, mix)
    return raw, jnp.swapaxes(smooth, 1, 2)


VMEM_GRANT = 60 * 2**20
GRADIENT_GRANT = 55 * 2**20
MIX_GRANT = 56 * 2**20


def solution(mesh):
    step = jax.shard_map(
        per_device,
        mesh=mesh,
        in_specs=(
            P(("parts", "mp"), None, None),
            P(("parts", "shot"), "mp", None, None),
            P(("parts", "shot"), "mp", None, None),
            P(("parts", "shot"), "mp", None, None),
            P(("parts", "shot"), "mp", None, None),
            P(("parts", "shot"), None),
            P(("parts", "shot"), None),
            P(("parts", "shot"), None, None),
            P("parts"),
            P(("parts", "shot"), None, None),
        ),
        out_specs=(P(("parts", "mp"), "shot", None), P(("parts", "shot"), None, "mp")),
        check_vma=False,
    )
    return step
```

```python
import math

import jax
import jax.numpy as jnp
import numpy as np
from jax import lax
from jax.experimental import pallas as pl
from jax.experimental.pallas import tpu as pltpu
from jax.sharding import PartitionSpec as P

SMOOTH_X = 32
SMOOTH_YZ = 4
COEFS = (8.0 / 5.0, -1.0 / 5.0, 8.0 / 315.0, -1.0 / 560.0)
CENTER = -205.0 / 72.0
REACH = 4
HIGHEST = lax.Precision.HIGH
MESH = pl.DeviceIdType.MESH

SCALE = 5040.0
WHOLE = tuple(float(round(SCALE * weight)) for weight in COEFS)
MIDDLE = 3.0 * float(round(SCALE * CENTER))

VMEM = pl.BlockSpec(memory_space=pltpu.VMEM)
SMEM = pl.BlockSpec(memory_space=pltpu.SMEM)
HBM = pl.BlockSpec(memory_space=pltpu.HBM)


def smoothing_table(length, strength):
    counter = np.arange(1, length + 1, dtype=np.float64)
    sines = np.sin(np.pi * np.outer(counter, counter) / (length + 1))
    half_sine = np.sin(np.pi * counter / (2 * (length + 1)))
    resp = 1.0 / (1.0 + strength * 4.0 * half_sine**2)
    table = 2.0 / (length + 1) * (sines * resp[None, :]) @ sines
    return table, 1.0 / math.sqrt(np.mean(resp * resp))


def stencil_tables(width_y, width_z):
    def bands(length):
        return sum(
            weight * (np.eye(length, k=offset + 1) + np.eye(length, k=-offset - 1))
            for offset, weight in enumerate(WHOLE)
        )

    band_y = bands(width_y)
    band_z = np.kron(np.eye(2), bands(width_z))
    return (
        jnp.asarray(np.concatenate([band_y, band_y], axis=1), jnp.bfloat16),
        jnp.asarray(np.concatenate([band_z, band_z], axis=0), jnp.bfloat16),
    )


def split(cell, width):
    if width & (width - 1) == 0:
        return cell >> (width.bit_length() - 1), cell & (width - 1)
    return lax.div(cell, width), lax.rem(cell, width)


def inject_kernel(
    packed, rec_data, src_sign, wavelet, late, now,
    late_out, now_out, first_out, second_out,
    late_buf, now_buf, first_buf, second_buf,
    cells, rec_values, src_signs, src_values, picks, sems,
):
    size, width = math.prod(late.shape), late.shape[1]
    rows = size // width
    bits = cell_bits(size, width)
    whole = pl.ds(0, rows)
    moves = [
        (packed, cells), (rec_data, rec_values), (src_sign, src_signs), (wavelet, src_values),
        (late, late_buf.at[whole]), (now, now_buf.at[whole]),
        (first_buf.at[whole], first_out), (second_buf.at[whole], second_out),
        (late_buf.at[whole], late_out), (now_buf.at[whole], now_out),
    ]
    copies = [
        pltpu.make_async_copy(source, target, sems.at[index])
        for index, (source, target) in enumerate(moves)
    ]
    for copy in copies[:6]:
        copy.start()
    step = math.gcd(rows, 256)

    def clear(index, carry):
        place = pl.ds(pl.multiple_of(index * step, step), step)
        zero = jnp.zeros((step, width), jnp.float32)
        first_buf[place, :] = zero
        second_buf[place, :] = zero
        return carry

    lax.fori_loop(0, rows // step, clear, 0)
    lanes = lax.broadcasted_iota(jnp.int32, (1, width), 1)
    group = GROUP

    def choose(start, total):
        together = math.gcd(total, 8)

        def some(index, count):
            values = [cells[start + index * together + extra] for extra in range(together)]
            grows = [1 + (value >> 31) for value in values]
            for value, grow in zip(values, grows):
                picks[count] = value
                count += grow
            return count

        count = lax.fori_loop(0, total // together, some, 0)
        for extra in range(2 * group - 1):
            picks[count + extra] = size
        return count

    def add(count, amounts, outs, sign):
        def fetch(index):
            values = [picks[index * group + extra] for extra in range(group)]
            amount = tuple(amounts(value >> bits) for value in values)
            local = [value & ((1 << bits) - 1) for value in values]
            return tuple(split(cell, width) for cell in local), amount

        def some(index, carry):
            spots, amount = carry
            places, lane = zip(*spots)
            olds = [[out[pl.ds(place, 1), :] for place in places] for out in outs]
            masks = [lanes == column for column in lane]
            added = [
                [jnp.where(mask, pair[side], 0.0) for mask, pair in zip(masks, amount)]
                for side in range(len(outs))
            ]
            totals = [list(parts) for parts in added]
            for later in range(group):
                for early in range(later):
                    same = places[early] == places[later]
                    for side in range(len(outs)):
                        totals[side][later] += jnp.where(same, added[side][early], 0.0)
            for side, out in enumerate(outs):
                for place, old, total in zip(places, olds[side], totals[side]):
                    out[pl.ds(place, 1), :] = old + total if sign > 0 else old - total
            return fetch(index + 1)

        lax.fori_loop(0, lax.div(count + (group - 1), group), some, fetch(0))

    def source_values(item):
        sign = (2 * src_signs[0, item] - 1).astype(jnp.float32)
        return sign * src_values[0, 0, item], sign * src_values[0, 1, item]

    receivers, sources = rec_data.shape[-1], src_sign.shape[-1]
    for copy in copies[:4]:
        copy.wait()
    add(choose(receivers, sources), source_values, (first_buf, second_buf), 1)
    copies[6].start()
    copies[7].start()
    count = choose(0, receivers)
    copies[4].wait()
    copies[5].wait()
    add(count, lambda item: (rec_values[0, 0, item], rec_values[0, 1, item]), (late_buf, now_buf), -1)
    copies[8].start()
    copies[9].start()
    for copy in copies[6:]:
        copy.wait()


GROUP = 4


def cell_bits(size, width):
    return (size + width - 1).bit_length()


def inject(rec_cell, rec_data, src_cell, src_sign, wavelet, late, now):
    size, width = math.prod(late.shape), late.shape[1]
    bits = cell_bits(size, width)
    receivers, sources = rec_cell.shape[0], src_cell.shape[1]
    most = max(receivers, sources)
    assert bits + (most - 1).bit_length() <= 31
    items = np.concatenate([np.arange(receivers), np.arange(sources)]).astype(np.int32) << bits
    local = jnp.concatenate([rec_cell, src_cell[0]]) - lax.axis_index("mp") * size
    packed = jnp.where((local >= 0) & (local < size), local | items, -1)
    shape = jax.ShapeDtypeStruct(late.shape, jnp.float32)
    padded = pltpu.VMEM((late.shape[0] + 8, width), jnp.float32)
    small = (packed, rec_data, src_sign, wavelet)
    return pl.pallas_call(
        inject_kernel,
        out_shape=(shape,) * 4,
        in_specs=[HBM] * 6,
        out_specs=(HBM,) * 4,
        scratch_shapes=[padded] * 4
        + [pltpu.SMEM(array.shape, array.dtype) for array in small]
        + [pltpu.SMEM((most + 2 * GROUP,), jnp.int32), pltpu.SemaphoreType.DMA((10,))],
        compiler_params=pltpu.CompilerParams(vmem_limit_bytes=VMEM_GRANT),
        name="inject",
    )(*small, late, now)


def slab_tables(table, count, order):
    rows = table.shape[0] // count
    mixes, sums = [], []
    for me in range(count):
        own = slice(me * rows, (me + 1) * rows)
        sums.append(np.stack([table[me * rows, own][order], table[(me + 1) * rows - 1, own][order]]))
        columns = [table[own, own][:, order]]
        for shift in range(1, count):
            source = (me - shift) % count
            seen = (source + 1) * rows - 1 if source < me else source * rows
            columns.append((table[own, seen] / table[seen, seen])[:, None])
        mixes.append(np.concatenate(columns, axis=1))
    return (
        jnp.asarray(np.stack(mixes).reshape(-1), jnp.float32),
        jnp.asarray(np.stack(sums).reshape(-1), jnp.float32),
    )


def make_kernel(slabs, groups, rows, width_y, width_z):
    blocks = rows // REACH
    chips = groups // 2
    lines = width_y // groups
    lanes = max(lines, min(128, REACH * lines))
    group = lanes // lines
    ratio = slabs // groups
    deep = width_z // slabs
    parts = ((rows - 2 * REACH) // group, 2 * REACH // group)
    starts = (0, parts[0])
    total_places = sum(parts)
    total_rows = ratio * rows
    ready_planes = slabs * total_places * deep * lanes // (width_y * width_z)

    def kernel(
        f_hbm, a_hbm, old_hbm, courant_hbm, late_hbm, now_hbm, first_hbm, second_hbm,
        table_y, table_z, smooth_y, smooth_z, sums,
        raw_out, lined, planes_in,
        raw, fbuf, abuf, obuf, cbuf, nbuf, mbuf, lbuf, sbuf, halo_one, halo_two,
        pair_in, chip_in, arrived, spread, planes,
        load_sem, one_send, one_recv, two_send, two_recv, pair_send, pair_recv,
        chip_send, chip_recv, turn_send, turn_recv, plane_send, plane_recv,
    ):
        m, s = lax.axis_index("mp"), lax.axis_index("shot")
        core = lax.rem(s, 2)
        chip = lax.div(s, 2)
        exists = (m > 0, m < slabs - 1)
        beside = (m - 1, m + 1)
        partner = s + 1 - 2 * core

        inner = list(range(2, blocks - 2))
        near = [block for block in (1, blocks - 2) if 0 < block < blocks - 1]
        near = sorted(set(near) - set(inner))
        edges = [0, blocks - 1]

        barrier = pltpu.get_barrier_semaphore()
        peers = slabs * groups
        me = m * groups + s

        def greet(index, carry):
            other = lax.rem(me + index, peers)
            pl.semaphore_signal(
                barrier, inc=1,
                device_id={"mp": lax.div(other, groups), "shot": lax.rem(other, groups)},
                device_id_type=MESH,
            )
            return carry

        lax.fori_loop(1, peers, greet, 0)

        term = abuf.reshape(rows + 2 * REACH, chips, 2, lines, width_z)
        pair = fbuf.at[: rows // 2].reshape(rows, chips, lines, width_z)
        ready = fbuf.at[rows // 2 : rows // 2 + ready_planes].reshape(slabs, total_places, deep, lanes)
        buffers = (
            (f_hbm, fbuf, REACH), (a_hbm, abuf, REACH), (old_hbm, obuf, 0), (courant_hbm, cbuf, 0),
            (late_hbm, lbuf, 0), (first_hbm, sbuf, 0), (now_hbm, lbuf, 0), (second_hbm, sbuf, 0),
        )

        def load(which, block):
            source, target, pad = buffers[which]
            return pltpu.make_async_copy(
                source.at[pl.ds(block * REACH, REACH)],
                target.at[pl.ds(block * REACH + pad, REACH)],
                load_sem.at[which, block],
            )

        for block in range(blocks):
            for which in range(6):
                load(which, block).start()
        for buf in (fbuf, abuf, nbuf, mbuf):
            zero = jnp.zeros((REACH,) + buf.shape[1:], jnp.float32)
            buf[:REACH] = zero
            buf[REACH + rows :] = zero

        pl.semaphore_wait(barrier, peers - 1)

        def one_copy(side, field, reach):
            row = reach if side == 0 else rows - 1 - reach
            return pltpu.make_async_remote_copy(
                src_ref=(f_hbm, a_hbm)[field].at[row],
                dst_ref=halo_one.at[1 - side, field, reach],
                send_sem=one_send.at[side, field, reach],
                recv_sem=one_recv.at[1 - side, field, reach],
                device_id={"mp": beside[side]},
                device_id_type=MESH,
            )

        def two_copy(side, field, reach):
            row = reach if side == 0 else rows - 1 - reach
            return pltpu.make_async_remote_copy(
                src_ref=(nbuf, mbuf)[field].at[REACH + row],
                dst_ref=halo_two.at[1 - side, field, reach],
                send_sem=two_send.at[side, field, reach],
                recv_sem=two_recv.at[1 - side, field, reach],
                device_id={"mp": beside[side]},
                device_id_type=MESH,
            )

        def landed(buffer, sem, side, field, reach):
            ref = buffer.at[side, field, reach]
            return pltpu.make_async_copy(ref, ref, sem.at[side, field, reach])

        for side in range(2):

            @pl.when(exists[side])
            def _():
                for reach in range(REACH):
                    for field in range(2):
                        one_copy(side, field, reach).start()

        spread[...] = jnp.zeros(spread.shape, jnp.float32)
        for source in range(groups):
            for part in range(group):
                top = source * lanes + part * lines
                spread[top : top + lines, part * width_y : (part + 1) * width_y] = smooth_y[
                    source * lines : (source + 1) * lines, :
                ]

        def laplace(place, fields):
            centers = [field[place] for field in fields]
            both = jnp.concatenate(centers, axis=1)
            high = both.astype(jnp.bfloat16)
            low = (both - high.astype(jnp.float32)).astype(jnp.bfloat16)
            total = jnp.dot(
                table_y[...], jnp.concatenate([high, low], axis=0), preferred_element_type=jnp.float32
            ) + jnp.dot(
                jnp.concatenate([high, low], axis=1), table_z[...], preferred_element_type=jnp.float32
            )
            laps = []
            for side, field in enumerate(fields):
                lap = total[:, side * width_z : (side + 1) * width_z] + MIDDLE * centers[side]
                for offset, weight in enumerate(WHOLE):
                    lap += weight * (field[place + offset + 1] + field[place - offset - 1])
                laps.append(lap)
            return centers, laps

        def first_block(block, carry):
            @pl.when(block + 1 < blocks)
            def _():
                for which in range(6):
                    load(which, block + 1).wait()

            for extra in range(REACH):
                row = block * REACH + extra
                (f_row, a_row), (lap_f, lap_a) = laplace(row + REACH, (fbuf, abuf))
                here = cbuf[row] * (1.0 / SCALE)
                accel = here * lap_f + sbuf[row]
                nbuf[row + REACH] = (2.0 * f_row - obuf[row]) + accel
                obuf[row] = accel
                mbuf[row + REACH] = (2.0 * a_row - lbuf[row]) + here * lap_a
            return carry

        for which in range(6):
            load(which, 0).wait()
        lax.fori_loop(0, blocks, first_block, 0)
        for block in inner + near + edges:
            for which in (6, 7):
                load(which, block).start()

        def first_edge(reach):
            for side in range(2):

                @pl.when(exists[side])
                def _():
                    for field in range(2):
                        landed(halo_one, one_recv, side, field, reach).wait()
                    for near in range(REACH - reach):
                        row = near if side == 0 else rows - 1 - near
                        here = COEFS[reach + near] * cbuf[row]
                        add_f = here * halo_one[side, 0, reach]
                        obuf[row] += add_f
                        nbuf[row + REACH] += add_f
                        mbuf[row + REACH] += here * halo_one[side, 1, reach]
                    for field in range(2):
                        two_copy(side, field, REACH - 1 - reach).start()

        def second_block(block):
            for which in (6, 7):
                load(which, block).wait()
            for extra in range(REACH):
                row = block * REACH + extra
                (_, a_row), (lap_f, lap_a) = laplace(row + REACH, (nbuf, mbuf))
                here = cbuf[row] * (1.0 / SCALE)
                accel_second = here * lap_f + sbuf[row]
                a_first = (2.0 * a_row - lbuf[row]) + here * lap_a
                value = a_first * obuf[row] + a_row * accel_second
                term[row] = value.reshape(chips, 2, lines, width_z)

        def pair_copy(block):
            return pltpu.make_async_remote_copy(
                src_ref=term.at[pl.ds(block * REACH, REACH), :, 1 - core],
                dst_ref=pair_in.at[pl.ds(block * REACH, REACH)],
                send_sem=pair_send.at[block],
                recv_sem=pair_recv.at[block],
                device_id={"shot": partner},
                device_id_type=MESH,
            )

        def chip_copy(shift, block):
            other = lax.rem(chip + shift, chips)
            return pltpu.make_async_remote_copy(
                src_ref=pair.at[pl.ds(block * REACH, REACH), other],
                dst_ref=chip_in.at[shift - 1, pl.ds(block * REACH, REACH)],
                send_sem=chip_send.at[shift - 1, block],
                recv_sem=chip_recv.at[shift - 1, block],
                device_id={"shot": other * 2 + core},
                device_id_type=MESH,
            )

        def add_pair(block):
            pair_copy(block).wait_recv()
            here = pl.ds(block * REACH, REACH)
            pair[here] = term[here, :, core] + pair_in[here]
            for shift in range(1, chips):
                chip_copy(shift, block).start()

        def add_chips(block):
            here = pl.ds(block * REACH, REACH)
            value = pair[here, chip]
            for shift in range(1, chips):
                chip_copy(shift, block).wait_recv()
                value += chip_in[shift - 1, here]
            raw[here] = value / float(groups)

        def turn_rows(start, count, place):
            turned = lax.dot_general(
                smooth_z[...],
                raw[start : start + count].reshape(count * lines, width_z),
                (((1,), (1,)), ((), ())),
                precision=HIGHEST,
                preferred_element_type=jnp.float32,
            )
            for index in range(count // group):
                for target in range(slabs):
                    ready[target, place + index] = turned[
                        target * deep : (target + 1) * deep, index * lanes : (index + 1) * lanes
                    ]

        goal = lax.div(m, ratio)
        slot = lax.rem(m, ratio) * groups + s

        def turn_copy(part, shift):
            target = lax.rem(m + shift, slabs)
            place = pl.ds(starts[part], parts[part])
            return pltpu.make_async_remote_copy(
                src_ref=ready.at[target, place],
                dst_ref=arrived.at[slot, place],
                send_sem=turn_send.at[part, target],
                recv_sem=turn_recv.at[part, slot],
                device_id={"mp": target, "shot": goal},
                device_id_type=MESH,
            )

        def turn_start(part):
            for shift in range(1, slabs):
                turn_copy(part, shift).start()

            @pl.when(s != goal)
            def _():
                turn_copy(part, 0).start()

            @pl.when(s == goal)
            def _():
                place = pl.ds(starts[part], parts[part])
                pltpu.make_async_copy(
                    ready.at[m, place], arrived.at[slot, place], turn_recv.at[part, slot]
                ).start()

        def turn_wait(part):
            place = pl.ds(starts[part], parts[part])
            for index in range(ratio * groups):
                ref = arrived.at[index, place]
                pltpu.make_async_copy(ref, ref, turn_recv.at[part, index]).wait()

        first_edge(0)
        first_edge(1)
        for block in inner:
            second_block(block)
            pair_copy(block).start()
        first_edge(2)
        for block in inner:
            add_pair(block)
        first_edge(3)
        for block in near:
            second_block(block)
            pair_copy(block).start()
        for block in edges:
            second_block(block)
        for block in near:
            add_pair(block)
        for block in inner + near:
            add_chips(block)
        turn_rows(REACH, rows - 2 * REACH, 0)

        for reach in reversed(range(REACH)):
            for side in range(2):

                @pl.when(exists[side])
                def _():
                    for field in range(2):
                        landed(halo_two, two_recv, side, field, reach).wait()
                    for close in range(REACH - reach):
                        row = close if side == 0 else rows - 1 - close
                        here = COEFS[reach + close] * cbuf[row]
                        extra = halo_two[side, 1, reach] * obuf[row] + mbuf[row + REACH] * halo_two[side, 0, reach]
                        term[row] += (here * extra).reshape(chips, 2, lines, width_z)

        for block in edges:
            pair_copy(block).start()
        turn_start(0)
        for block in edges:
            add_pair(block)
        for block in edges:
            add_chips(block)
        turn_rows(0, REACH, parts[0])
        turn_rows(rows - REACH, REACH, parts[0] + REACH // group)
        turn_start(1)
        raw_copy = pltpu.make_async_copy(raw, raw_out, load_sem.at[0, 0])
        raw_copy.start()

        turn_wait(0)
        turn_wait(1)
        for index in range(ratio):
            joined = jnp.concatenate(
                [
                    arrived[index * groups + source].reshape(total_places * deep, lanes)
                    for source in range(groups)
                ],
                axis=1,
            )
            done = jnp.dot(joined, spread[...], precision=HIGHEST, preferred_element_type=jnp.float32)
            for place in range(total_places):
                for part in range(group):
                    lined[(index * total_places + place) * group + part] = done[
                        place * deep : (place + 1) * deep, part * width_y : (part + 1) * width_y
                    ]
        base = s * (2 * total_rows)
        for side in range(2):
            sum_side = sums[base + side * total_rows] * lined[0]
            for row in range(1, total_rows):
                sum_side += sums[base + side * total_rows + row] * lined[row]
            planes[side] = sum_side

        def plane_copy(shift):
            upward = jnp.where(s + shift < groups, 1, 0)
            return pltpu.make_async_remote_copy(
                src_ref=planes.at[upward],
                dst_ref=planes_in.at[shift - 1],
                send_sem=plane_send.at[shift - 1],
                recv_sem=plane_recv.at[shift - 1],
                device_id={"shot": lax.rem(s + shift, groups)},
                device_id_type=MESH,
            )

        for shift in range(1, groups):
            plane_copy(shift).start()
        for shift in range(1, groups):
            plane_copy(shift).wait_recv()
        for side in range(2):

            @pl.when(exists[side])
            def _():
                for reach in range(REACH):
                    for field in range(2):
                        one_copy(side, field, reach).wait_send()
                        two_copy(side, field, reach).wait_send()

        for block in range(blocks):
            pair_copy(block).wait_send()
            for shift in range(1, chips):
                chip_copy(shift, block).wait_send()
        for part in range(2):
            for shift in range(1, slabs):
                turn_copy(part, shift).wait_send()

            @pl.when(s != goal)
            def _():
                turn_copy(part, 0).wait_send()

        for shift in range(1, groups):
            plane_copy(shift).wait_send()
        raw_copy.wait()

    padded = pltpu.VMEM((rows + 2 * REACH, width_y, width_z), jnp.float32)
    slab = pltpu.VMEM((rows, width_y, width_z), jnp.float32)
    halo = pltpu.VMEM((2, 2, REACH, width_y, width_z), jnp.float32)
    dma = pltpu.SemaphoreType.DMA
    scratch = [
        pltpu.VMEM((rows, lines, width_z), jnp.float32),
        padded, padded, slab, slab, padded, padded, slab, slab,
        halo, halo,
        pltpu.VMEM((rows, chips, lines, width_z), jnp.float32),
        pltpu.VMEM((max(1, chips - 1), rows, lines, width_z), jnp.float32),
        pltpu.VMEM((ratio * groups, total_places, deep, lanes), jnp.float32),
        pltpu.VMEM((groups * lanes, group * width_y), jnp.float32),
        pltpu.VMEM((2, deep, width_y), jnp.float32),
        dma((8, blocks)),
        dma((2, 2, REACH)), dma((2, 2, REACH)), dma((2, 2, REACH)), dma((2, 2, REACH)),
        dma((blocks,)), dma((blocks,)),
        dma((max(1, chips - 1), blocks)), dma((max(1, chips - 1), blocks)),
        dma((2, slabs)), dma((2, ratio * groups)),
        dma((groups - 1,)), dma((groups - 1,)),
    ]
    outs = (
        jax.ShapeDtypeStruct((rows, lines, width_z), jnp.float32),
        jax.ShapeDtypeStruct((total_rows, deep, width_y), jnp.float32),
        jax.ShapeDtypeStruct((groups - 1, deep, width_y), jnp.float32),
    )
    inner_rows = list(range(REACH, rows - REACH)) + list(range(REACH)) + list(range(rows - REACH, rows))
    order = np.concatenate([index * rows + np.array(inner_rows) for index in range(ratio)])
    return kernel, scratch, outs, order


def mix_kernel(
    raw_hbm, lined, planes, mix, raw_out, smooth, raw, buffer, sems
):
    total_rows, others = lined.shape[0], planes.shape[0]
    wide = total_rows + others
    step = math.gcd(total_rows, 4)
    base = lax.axis_index("shot") * total_rows
    fetch = pltpu.make_async_copy(raw_hbm, raw, sems.at[0])
    fetch.start()
    store = pltpu.make_async_copy(raw, raw_out, sems.at[1])

    def write(index):
        here = pl.ds(index * step, step)
        return pltpu.make_async_copy(buffer.at[here], smooth.at[here], sems.at[index + 2])

    def some(index, carry):
        totals = [None] * step
        for source in range(wide):
            value = lined[source] if source < total_rows else planes[source - total_rows]
            for extra in range(step):
                piece = mix[(base + index * step + extra) * wide + source] * value
                totals[extra] = piece if source == 0 else totals[extra] + piece
        for extra in range(step):
            buffer[index * step + extra] = totals[extra]
        write(index).start()
        return carry

    half = total_rows // step // 2
    lax.fori_loop(0, half, some, 0)
    fetch.wait()
    store.start()
    lax.fori_loop(half, total_rows // step, some, 0)
    for index in range(total_rows // step):
        write(index).wait()
    store.wait()


def mix_planes(raw, lined, planes, mix):
    steps = lined.shape[0] // math.gcd(lined.shape[0], 4)
    return pl.pallas_call(
        mix_kernel,
        out_shape=(
            jax.ShapeDtypeStruct(raw.shape, jnp.float32),
            jax.ShapeDtypeStruct(lined.shape, jnp.float32),
        ),
        in_specs=[HBM, VMEM, VMEM, SMEM],
        out_specs=(HBM, HBM),
        scratch_shapes=[
            pltpu.VMEM(raw.shape, jnp.float32), pltpu.VMEM(lined.shape, jnp.float32),
            pltpu.SemaphoreType.DMA((steps + 2,)),
        ],
        compiler_params=pltpu.CompilerParams(vmem_limit_bytes=MIX_GRANT),
        name="mix",
    )(raw, lined, planes, mix)


def per_device(
    courant, forward_old, forward_now, adjoint_late, adjoint_now,
    src_cell, src_sign, wavelet, rec_cell, rec_data,
):
    rows, width_y, width_z = courant.shape
    slabs, groups = lax.axis_size("mp"), lax.axis_size("shot")
    flat = (rows * width_y, width_z)
    injected = inject(
        rec_cell, rec_data, src_cell, src_sign, wavelet,
        adjoint_late.reshape(flat), adjoint_now.reshape(flat),
    )
    kernel, scratch, outs, order = make_kernel(slabs, groups, rows, width_y, width_z)
    table_x, spread_x = smoothing_table(rows * slabs, SMOOTH_X**2)
    smooth_y, spread_y = smoothing_table(width_y, SMOOTH_YZ**2)
    smooth_z, spread_z = smoothing_table(width_z, SMOOTH_YZ**2)
    smooth_y = smooth_y * (spread_x * spread_y * spread_z)
    mix, sums = slab_tables(table_x, groups, order)
    raw, lined, planes = pl.pallas_call(
        kernel,
        out_shape=outs,
        in_specs=[HBM] * 8 + [VMEM] * 4 + [SMEM],
        out_specs=(HBM, VMEM, VMEM),
        scratch_shapes=scratch,
        compiler_params=pltpu.CompilerParams(
            collective_id=0, has_side_effects=True, vmem_limit_bytes=GRADIENT_GRANT
        ),
        name="gradient",
    )(
        forward_now[0], adjoint_now[0], forward_old[0], courant,
        *(array.reshape(rows, width_y, width_z) for array in injected),
        *stencil_tables(width_y, width_z),
        jnp.asarray(smooth_y, jnp.float32), jnp.asarray(smooth_z, jnp.float32),
        sums,
    )
    raw, smooth = mix_planes(raw, lined, planes, mix)
    return raw, jnp.swapaxes(smooth, 1, 2)


VMEM_GRANT = 60 * 2**20
GRADIENT_GRANT = 55 * 2**20
MIX_GRANT = 56 * 2**20


def solution(mesh):
    step = jax.shard_map(
        per_device,
        mesh=mesh,
        in_specs=(
            P(("parts", "mp"), None, None),
            P(("parts", "shot"), "mp", None, None),
            P(("parts", "shot"), "mp", None, None),
            P(("parts", "shot"), "mp", None, None),
            P(("parts", "shot"), "mp", None, None),
            P(("parts", "shot"), None),
            P(("parts", "shot"), None),
            P(("parts", "shot"), None, None),
            P("parts"),
            P(("parts", "shot"), None, None),
        ),
        out_specs=(P(("parts", "mp"), "shot", None), P(("parts", "shot"), None, "mp")),
        check_vma=False,
    )
    return step
```
